32 devices in a mesh: dp: 16 (over z, y, x), tensor: 2 (over core).
Axes of the slice: x: 2, y: 2, z: 4, core: 2. Of those that a mesh axis runs over, the one named last changes fastest.
Arguments:
- tokens: bfloat16 [8192, 1024], P('dp', 'tensor'), may hold values from -6 to 6
- norm_gains: float32 [2, 1024], replicated, may hold values from 0.5 to 1.5
- qkv_weight: bfloat16 [1024, 3, 1024], P(None, None, 'tensor'), may hold values from -0.1875 to 0.1875
- conv_weight: float32 [4, 3, 1024], P(None, None, 'tensor'), may hold values from -2 to 2
- log_decay: float32 [16, 8, 512], P('dp', 'tensor'), may hold values from -1 to 0
- regular: float32 [8, 128], P('tensor'), may hold values from 0.25 to 1
- out_weight: bfloat16 [1024, 1024], P('tensor'), may hold values from -0.1875 to 0.1875
- gate_up_weight: bfloat16 [1024, 2, 1536], P(None, None, 'tensor'), may hold values from -0.1875 to 0.1875
- down_weight: bfloat16 [1536, 1024], P('tensor'), may hold values from -0.15625 to 0.15625
- prefix_cache: float32 [16, 8, 2, 128, 128], P('dp', 'tensor'), as said below
- prefix_tail: float32 [16, 3, 3, 1024], P('dp', None, None, 'tensor'), may hold values from -6 to 6
- suffix_len: int32 [16], P('dp'), may hold values from 1 to 512, as said below
- request_group: int32 [16], P('dp'), may hold values from 0 to 3
- prefix_owner: int32 [4], replicated, may hold values from 0 to 15, as said below
Outputs:
- mixed: bfloat16 [8192, 1024], P('dp', 'tensor')
- final_state: float32 [16, 8, 2, 128, 128], P('dp', 'tensor')
- final_tail: float32 [16, 3, 3, 1024], P('dp', None, None, 'tensor')
The draws below stay inside these ranges and needn't reach their ends.
Inputs may be any that keep to these rules, and one draw needn't show every extreme that they name: `suffix_len`: every request has 1 to 512 live rows; in every draw one request has exactly 512. `prefix_owner`: the owners of the groups are distinct slots. prefix_cache[s, h, 0] is symmetric positive definite.
All inputs are finite; a program needn't handle non-finite values.
Results may differ from the reference program's by a relative error of at most 0.0067.
Values may be sent and summed in bfloat16 or wider, within the bound.
No kernel may reach another device: no remote copies, remote signals or barrier semaphores. Data moves between devices by JAX's collectives and lax.ppermute only.
A program may use at most 128 MiB of HBM per device.

```python
import math
import jax
import jax.numpy as jnp
from jax import lax

D = 1024
HEAD_COUNT = 8
DK = 128
FF = 1536
CONV = 4
BLOCK = 128
ITERS = 4
GROUPS = 4
SUFFIX_ROWS = 512
TOKENS = 8192
N_DP = 16


def draw_prefix_cache(key, part):
    random_subkeys = jax.random.split(key, 7)
    head_scale = jnp.exp(jax.random.uniform(random_subkeys[0], (N_DP, HEAD_COUNT, 1, 1), minval=jnp.log(0.5), maxval=jnp.log(20.0)))
    diag_scale = jnp.exp(jax.random.uniform(random_subkeys[1], (N_DP, HEAD_COUNT, DK), minval=jnp.log(0.05), maxval=0.0))
    entries = jax.random.uniform(random_subkeys[2], (N_DP, HEAD_COUNT, DK, DK), minval=-1.0, maxval=1.0)
    identity_mat = jnp.eye(DK, dtype=jnp.float32)
    coupling = (entries + jnp.swapaxes(entries, 2, 3)) * (0.45 / DK) * (1.0 - identity_mat)
    order_keys = jax.random.split(random_subkeys[5], N_DP * HEAD_COUNT)
    order = jax.vmap(lambda single: jax.random.permutation(single, DK))(order_keys).reshape(N_DP, HEAD_COUNT, DK)
    distance = jnp.abs(order[..., :, None] - order[..., None, :]).astype(jnp.float32)
    kernel = jnp.exp(-distance / 4.0)
    signs = jnp.where(jax.random.randint(random_subkeys[6], (N_DP, HEAD_COUNT, DK), 0, 2) == 0, -1.0, 1.0).astype(jnp.float32)
    banded = signs[..., :, None] * kernel * signs[..., None, :]
    mixture = 0.4 * (identity_mat + coupling) + 0.6 * banded
    diag_root = jnp.sqrt(diag_scale)
    gram_part = head_scale * diag_root[..., :, None] * mixture * diag_root[..., None, :]
    assoc_raw = jax.random.normal(random_subkeys[3], (N_DP, HEAD_COUNT, DK, DK)) * 0.3
    assoc_part = head_scale * assoc_raw
    return jnp.stack([gram_part, assoc_part], axis=2).astype(jnp.float32)


def draw_log_decay(key, part):
    random_subkeys = jax.random.split(key, 5)
    rate_low = jnp.log(0.2 / SUFFIX_ROWS)
    rate_high = jnp.log(1.0 / 30.0)
    logarithm_rate = jax.random.uniform(random_subkeys[0], (N_DP, HEAD_COUNT, 1), minval=rate_low, maxval=rate_high)
    request_multiplier = jnp.exp(jax.random.uniform(random_subkeys[1], (N_DP, 1, 1), minval=jnp.log(0.5), maxval=jnp.log(2.0)))
    random_offset = jax.random.uniform(random_subkeys[2], (N_DP, HEAD_COUNT, SUFFIX_ROWS), minval=0.5, maxval=1.5)
    spike_selected = jax.random.randint(random_subkeys[3], (N_DP, HEAD_COUNT, SUFFIX_ROWS), 0, SUFFIX_ROWS) < 8
    spike_length = jax.random.uniform(random_subkeys[4], (N_DP, HEAD_COUNT, SUFFIX_ROWS), minval=0.22, maxval=0.69)
    faded_value = -(jnp.exp(logarithm_rate) * request_multiplier * random_offset) - jnp.where(spike_selected, spike_length, 0.0)
    return faded_value.astype(jnp.float32)


def draw_suffix_len(key, part):
    random_subkeys = jax.random.split(key, 2)
    uniform_len = jax.random.randint(random_subkeys[0], (N_DP,), 1, SUFFIX_ROWS + 1)
    skewed = jnp.maximum(uniform_len * uniform_len // SUFFIX_ROWS, 1)
    longest = jax.random.randint(random_subkeys[1], (), 0, N_DP)
    return skewed.at[longest].set(SUFFIX_ROWS).astype(jnp.int32)


def draw_prefix_owner(key, part):
    return jax.random.permutation(key, N_DP)[:GROUPS].astype(jnp.int32)


def set_ends(values, own_key, least, largest):
    place = [jax.random.randint(jax.random.fold_in(own_key, axis), (), 0, length) for axis, length in enumerate(values.shape)]
    widest = values.shape.index(max(values.shape))
    beside = place[:widest] + [(place[widest] + 1) % values.shape[widest]] + place[widest + 1:]
    return values.at[tuple(place)].set(least).at[tuple(beside)].set(largest)


def levels(key, shape, cuts, low, largest):
    factor_of, own = 1.0, jax.random.fold_in(key, 6)
    for dim, parts in cuts:
        draws = jnp.exp(jax.random.uniform(jax.random.fold_in(own, dim), (parts,), jnp.float32, low / len(cuts), largest / len(cuts)))
        factor_of = factor_of * jnp.repeat(draws, shape[dim] // parts).reshape([-1 if axis == dim else 1 for axis in range(len(shape))])
    return factor_of


def scatter_about(own_key, dims, deviation, reach, pieces=(), kind=jnp.bfloat16):
    level = levels(own_key, dims, pieces, -0.22, 0.18) if pieces else 1.0
    values = jax.random.normal(own_key, dims, jnp.float32) * deviation * level
    return jnp.minimum(jnp.maximum(values, -reach), reach).astype(kind)


def setup_inputs(seed: int = 0) -> dict:
    keys = jax.random.split(jax.random.key(seed), 15)
    tokens = scatter_about(keys[0], (TOKENS, D), 1.0, 6.0, ((0, 16), (1, 2)))
    norm_gains = jnp.clip(1.0 + 0.1 * jax.random.normal(keys[1], (2, D), jnp.float32), 0.5, 1.5)
    qkv_weight = scatter_about(keys[2], (D, 3, HEAD_COUNT * DK), D ** -0.5, 0.1875, ((2, 2),))
    conv_weight = scatter_about(keys[3], (CONV, 3, HEAD_COUNT * DK), 0.5, 2.0, ((2, 2),), jnp.float32)
    log_decay = draw_log_decay(jax.random.fold_in(keys[14], 71), 0)
    regular = jnp.clip(jnp.exp(math.log(1.0) - 1.3862944 * jax.random.uniform(keys[5], (HEAD_COUNT, DK), jnp.float32) ** levels(keys[5], (HEAD_COUNT, DK), ((0, 2),), -0.2, 0.2)), 0.25, 1.0)
    out_weight = scatter_about(keys[6], (HEAD_COUNT * DK, D), (HEAD_COUNT * DK) ** -0.5, 0.1875, ((0, 2),))
    gate_up_weight = scatter_about(keys[7], (D, 2, FF), D ** -0.5, 0.1875, ((2, 2),))
    down_weight = scatter_about(keys[8], (FF, D), FF ** -0.5, 0.15625, ((0, 2),))
    prefix_cache = draw_prefix_cache(jax.random.fold_in(keys[14], 71), 0)
    prefix_tail = scatter_about(keys[10], (N_DP, CONV - 1, 3, HEAD_COUNT * DK), 1.0, 6.0, ((0, 16), (3, 2)), jnp.float32)
    suffix_len = draw_suffix_len(jax.random.fold_in(keys[14], 71), 0)
    request_group = set_ends(jax.random.randint(keys[12], (N_DP,), 0, GROUPS), jax.random.fold_in(keys[12], 1), 0, GROUPS - 1).astype(jnp.int32)
    prefix_owner = draw_prefix_owner(jax.random.fold_in(keys[14], 71), 0)
    return {"tokens": tokens, "norm_gains": norm_gains, "qkv_weight": qkv_weight, "conv_weight": conv_weight, "log_decay": log_decay, "regular": regular, "out_weight": out_weight, "gate_up_weight": gate_up_weight, "down_weight": down_weight, "prefix_cache": prefix_cache, "prefix_tail": prefix_tail, "suffix_len": suffix_len, "request_group": request_group, "prefix_owner": prefix_owner}


PRECISE = lax.Precision.HIGHEST

def rms_rows(values_in, gain):
    floats = values_in.astype(jnp.float32)
    inverse = lax.rsqrt(lax.optimization_barrier(jnp.mean(floats * floats, axis=-1, keepdims=True)) + 1e-05)
    return (floats * inverse * gain).astype(jnp.bfloat16)

def head_view(stacked):
    return stacked.reshape(stacked.shape[0], -1, DK).transpose(1, 0, 2)

def unit_heads(stacked):
    shaped = head_view(stacked)
    return shaped * lax.rsqrt(lax.optimization_barrier(jnp.sum(shaped * shaped, axis=-1, keepdims=True)) + 1e-06)

def mesa_block(queries, key_rows, value_rows, log_gate, hstate, gstate, regular):
    cumulative = jnp.cumsum(log_gate, axis=1)
    rows_count = log_gate.shape[1]
    causal_mask = jnp.arange(rows_count)[:, None] >= jnp.arange(rows_count)[None, :]
    differ = cumulative[:, :, None] - cumulative[:, None, :]
    weights = jnp.where(causal_mask[None], jnp.exp(jnp.minimum(differ, 0.0)), 0.0)
    growth = jnp.exp(cumulative)[:, :, None]

    def apply_op(search):
        through = jnp.einsum('hcd,hde->hce', search, hstate, precision=PRECISE)
        correlation = jnp.einsum('hcd,hid->hci', search, key_rows, precision=PRECISE) * weights
        local_part = jnp.einsum('hci,hid->hcd', correlation, key_rows, precision=PRECISE)
        return growth * through + local_part + regular[:, None, :] * search
    solved = jnp.zeros_like(queries)
    residual = queries
    search = queries
    norm_now = lax.optimization_barrier(jnp.sum(residual * residual, axis=-1, keepdims=True))
    for iteration in range(ITERS):
        applied = apply_op(search)
        step_size = norm_now / lax.optimization_barrier(jnp.sum(search * applied, axis=-1, keepdims=True))
        solved = solved + step_size * search
        residual = residual - step_size * applied
        norm_next = lax.optimization_barrier(jnp.sum(residual * residual, axis=-1, keepdims=True))
        search = residual + norm_next / norm_now * search
        norm_now = norm_next
    recall = jnp.einsum('hcd,hed->hce', solved, gstate, precision=PRECISE)
    correlation = jnp.einsum('hcd,hid->hci', solved, key_rows, precision=PRECISE) * weights
    output = growth * recall + jnp.einsum('hci,hie->hce', correlation, value_rows, precision=PRECISE)
    decay_tail = jnp.exp(cumulative[:, -1:] - cumulative)[:, :, None]
    decay_last = jnp.exp(cumulative[:, -1])[:, None, None]
    hstate_new = decay_last * hstate + jnp.einsum('hid,hie->hde', key_rows * decay_tail, key_rows, precision=PRECISE)
    gstate_new = decay_last * gstate + jnp.einsum('hie,hid->hed', value_rows * decay_tail, key_rows, precision=PRECISE)
    return (output, hstate_new, gstate_new)

def mixer(projected, conv_weight, tail_rows, log_gate, regular, state_pair, length, block_limit):
    rows_total = projected.shape[0]
    shaped = projected.reshape(rows_total, 3, -1)
    extended = jnp.concatenate([tail_rows, shaped], axis=0)
    convolved = conv_weight[0] * extended[0:rows_total]
    for tap_index in range(1, CONV):
        convolved = convolved + conv_weight[tap_index] * extended[tap_index:tap_index + rows_total]
    activated = jax.nn.silu(convolved)
    new_tail = lax.dynamic_slice_in_dim(extended, length.astype(jnp.int32), CONV - 1, 0)
    live_rows = jnp.arange(rows_total) < length
    queries = unit_heads(activated[:, 0])
    key_rows = jnp.where(live_rows[None, :, None], unit_heads(activated[:, 1]), 0.0)
    value_rows = jnp.where(live_rows[None, :, None], head_view(activated[:, 2]), 0.0)
    gate_logs = jnp.where(live_rows[None, :], log_gate, 0.0)

    def block_step(block_id, loop_state):
        hstate, gstate, heads_out = loop_state
        start_row = (block_id * BLOCK).astype(jnp.int32)

        def take_block(array_in):
            return lax.dynamic_slice_in_dim(array_in, start_row, BLOCK, 1)
        out_block, hstate, gstate = mesa_block(take_block(queries), take_block(key_rows), take_block(value_rows), take_block(gate_logs), hstate, gstate, regular)
        heads_out = lax.dynamic_update_slice_in_dim(heads_out, out_block, start_row, 1)
        return (hstate, gstate, heads_out)
    hstate, gstate, heads_out = lax.fori_loop(0, block_limit, block_step, (state_pair[:, 0], state_pair[:, 1], jnp.zeros_like(queries)))
    heads_flat = heads_out.transpose(1, 0, 2).reshape(rows_total, -1).astype(jnp.bfloat16)
    return (heads_flat, jnp.stack([hstate, gstate], axis=1), new_tail)

def reference(tokens, norm_gains, qkv_weight, conv_weight, log_decay, regular, out_weight, gate_up_weight, down_weight, prefix_cache, prefix_tail, suffix_len, request_group, prefix_owner):
    qkv_matrix = qkv_weight.reshape(D, -1)
    gate_matrix = gate_up_weight.reshape(D, -1)
    token_grid = tokens.reshape(N_DP, SUFFIX_ROWS, D)

    def one_request(request):
        owner_slot = prefix_owner[request_group[request]]
        length = suffix_len[request]
        rows_in = token_grid[request]
        projected = jnp.dot(rms_rows(rows_in, norm_gains[0]), qkv_matrix, preferred_element_type=jnp.float32)
        heads_flat, state_out, tail_out = mixer(projected, conv_weight, prefix_tail[owner_slot], log_decay[request], regular, prefix_cache[owner_slot], length, SUFFIX_ROWS // BLOCK)
        attended = jnp.dot(heads_flat, out_weight, preferred_element_type=jnp.float32)
        middle = (rows_in.astype(jnp.float32) + attended).astype(jnp.bfloat16)
        gate_up = jnp.dot(rms_rows(middle, norm_gains[1]), gate_matrix, preferred_element_type=jnp.float32).reshape(SUFFIX_ROWS, 2, -1)
        hidden = (jax.nn.silu(gate_up[:, 0]) * gate_up[:, 1]).astype(jnp.bfloat16)
        forward = jnp.dot(hidden, down_weight, preferred_element_type=jnp.float32)
        live_rows = jnp.arange(SUFFIX_ROWS) < length
        result = jnp.where(live_rows[:, None], middle.astype(jnp.float32) + forward, 0.0).astype(jnp.bfloat16)
        return (result, state_out, tail_out)
    results, states, tail_all = lax.map(one_request, jnp.arange(N_DP, dtype=jnp.int32))
    return (results.reshape(N_DP * SUFFIX_ROWS, D), states, tail_all)
```

```python
import functools

import jax
import jax.numpy as jnp
from jax import lax
from jax.experimental import pallas as pl
from jax.experimental.pallas import tpu as pltpu
from jax.sharding import PartitionSpec as P

DK = 128
CONV = 4
BLOCK = 128
ITERS = 4
LANES = 128
BF16 = jnp.bfloat16
F32 = jnp.float32


def rms_rows(floats, gain):
    inverse = lax.rsqrt(jnp.mean(floats * floats, axis=-1, keepdims=True) + 1e-05)
    return (floats * inverse * gain).astype(BF16)


def other_core(array_in):
    return lax.ppermute(array_in, "tensor", [(0, 1), (1, 0)])


def halves(value):
    high = value.astype(BF16)
    return high, (value - high.astype(F32)).astype(BF16)


def dot_nn(left, right):
    return lax.dot_general(left, right, (((1,), (0,)), ((), ())), preferred_element_type=F32)


def dot_nt(left, right):
    return lax.dot_general(left, right, (((1,), (1,)), ((), ())), preferred_element_type=F32)


def dot_tn(left, right):
    return lax.dot_general(left, right, (((0,), (0,)), ((), ())), preferred_element_type=F32)


def pack_kernel(group, cache, tail, packed):
    count, rows, _ = packed.shape
    heads = cache.shape[0]
    share = count // heads
    state_rows = rows - 8
    tail_rows = -(-(CONV - 1) * 3 // share)
    tag = jnp.full((1, LANES), group[0], jnp.int32).astype(F32)
    for head in range(heads):
        lanes = slice(head * DK, (head + 1) * DK)
        for piece in range(share):
            plane, offset = divmod(piece * state_rows, DK)
            parts = [cache[head, plane, offset : offset + state_rows, :]]
            for index in range(piece * tail_rows, (piece + 1) * tail_rows):
                if index < (CONV - 1) * 3:
                    parts.append(tail[index // 3, index % 3 : index % 3 + 1, lanes])
                else:
                    parts.append(tag)
            parts.append(jnp.broadcast_to(tag, (8 - tail_rows, LANES)))
            packed[head * share + piece] = jnp.concatenate(parts, axis=0).astype(BF16)


def pack(prefix_cache, prefix_tail, request_group, count):
    rows = prefix_cache.shape[0] * 2 * DK // count + 8
    return pl.pallas_call(
        pack_kernel,
        out_shape=jax.ShapeDtypeStruct((count, rows, LANES), BF16),
        in_specs=[
            pl.BlockSpec(memory_space=pltpu.SMEM),
            pl.BlockSpec(memory_space=pltpu.VMEM),
            pl.BlockSpec(memory_space=pltpu.VMEM),
        ],
        out_specs=pl.BlockSpec(memory_space=pltpu.VMEM),
        name="pack",
    )(request_group, prefix_cache, prefix_tail)


def route_kernel(owners, arrived, leaving):
    count, rows, _ = arrived.shape
    groups = owners.shape[0]
    held = [arrived[owners[group]].astype(F32) for group in range(groups)]

    def fill(slot, carry):
        wanted = arrived[slot].astype(F32)[rows - 1 : rows, :]
        chosen = held[0]
        for group in range(1, groups):
            chosen = jnp.where(wanted == float(group), held[group], chosen)
        leaving[slot] = chosen.astype(BF16)
        return carry

    lax.fori_loop(0, count, fill, 0)


def route(prefix_owner, arrived):
    return pl.pallas_call(
        route_kernel,
        out_shape=jax.ShapeDtypeStruct(arrived.shape, arrived.dtype),
        in_specs=[
            pl.BlockSpec(memory_space=pltpu.SMEM),
            pl.BlockSpec(memory_space=pltpu.VMEM),
        ],
        out_specs=pl.BlockSpec(memory_space=pltpu.VMEM),
        name="route",
    )(prefix_owner, arrived)


def mixer_kernel(
    length_ref,
    query_in,
    key_in,
    value_in,
    taps,
    prefix,
    decay,
    regular,
    out_weight,
    partial_out,
    state_out,
    tail_out,
    extended,
    total,
):
    rows_total = query_in.shape[1]
    blocks = rows_total // BLOCK
    head = pl.program_id(0)
    length = length_ref[0]
    share, chunk_rows, _ = prefix.shape
    state_rows = chunk_rows - 8
    tail_rows = -(-(CONV - 1) * 3 // share)
    chunks = [prefix[piece].astype(F32) for piece in range(share)]
    state = jnp.concatenate([chunk[:state_rows] for chunk in chunks], axis=0)
    hstate, gstate = state[:DK], state[DK:]

    live = lax.broadcasted_iota(jnp.int32, (rows_total, 1), 0) < length
    activated = []
    for part, source in enumerate((query_in, key_in, value_in)):
        for before in range(CONV - 1):
            piece, inside = divmod(before * 3 + part, tail_rows)
            place = state_rows + inside
            extended[5 + before : 6 + before, :] = chunks[piece][place : place + 1]
        extended[8 : 8 + rows_total, :] = source[0]
        convolved = taps[part, 0:1, :] * extended[pl.ds(5, rows_total), :]
        for tap in range(1, CONV):
            convolved = (
                convolved + taps[part, tap : tap + 1, :] * extended[pl.ds(5 + tap, rows_total), :]
            )
        tail_out[:, part, :] = extended[pl.ds(length + 5, CONV - 1), :]
        activated.append(convolved / (1.0 + jnp.exp(-convolved)))
    queries, key_rows, value_rows = activated
    queries = queries * lax.rsqrt(jnp.sum(queries * queries, axis=-1, keepdims=True) + 1e-06)
    key_rows = key_rows * lax.rsqrt(jnp.sum(key_rows * key_rows, axis=-1, keepdims=True) + 1e-06)
    key_rows = jnp.where(live, key_rows, 0.0)
    value_rows = jnp.where(live, value_rows, 0.0)

    lane = lax.broadcasted_iota(jnp.int32, (BLOCK, BLOCK), 1)
    row = lax.broadcasted_iota(jnp.int32, (BLOCK, BLOCK), 0)
    causal = row >= lane
    regular_row = regular[0]

    operands = []
    for block in range(blocks):
        rows = slice(block * BLOCK, (block + 1) * BLOCK)
        keys, values = key_rows[rows], value_rows[rows]
        gates = decay[0, :, block * BLOCK : (block + 1) * BLOCK]
        position = lax.broadcasted_iota(jnp.int32, (1, BLOCK), 1) + block * BLOCK
        gates = jnp.where(position < length, gates, 0.0)
        down = jnp.sum(jnp.where(causal, gates, 0.0), axis=1, keepdims=True)
        wide = jnp.broadcast_to(down, (BLOCK, BLOCK))
        differ = wide - wide.T
        weights = jnp.where(causal, jnp.exp(jnp.minimum(differ, 0.0)), 0.0)
        growth = jnp.exp(down)
        last = down[BLOCK - 1 : BLOCK, :]
        root_tail = jnp.exp(0.5 * (last - down))
        decay_last = jnp.exp(last)
        keys_high = keys.astype(BF16)
        operands.append(
            (
                keys_high,
                jnp.concatenate([hstate.astype(BF16), keys_high], axis=0),
                gstate.astype(BF16),
                values.astype(BF16),
                weights,
                growth,
            )
        )
        grown = jnp.concatenate([keys * root_tail, values * root_tail], axis=1).astype(BF16)
        update = dot_tn(grown, grown[:, :DK])
        hstate = decay_last * hstate + update[:DK]
        gstate = decay_last * gstate + update[DK:]
    state_out[0, 0] = hstate
    state_out[0, 1] = gstate

    search = [queries[block * BLOCK : (block + 1) * BLOCK] for block in range(blocks)]
    residual = list(search)
    solved = [None] * blocks
    correlated = [None] * blocks
    norm_now = [jnp.sum(r * r, axis=-1, keepdims=True) for r in residual]
    for iteration in range(ITERS):
        for block in range(blocks):
            k_high, mix_high, _, _, weights, growth = operands[block]
            p_now = search[block]
            p_high, p_low = halves(p_now)
            reach = (dot_nt(p_high, k_high) + dot_nt(p_low, k_high)) * weights
            b_high, b_low = halves(jnp.concatenate([growth * p_now, reach], axis=1))
            applied = dot_nn(b_high, mix_high) + dot_nn(b_low, mix_high) + regular_row * p_now
            step = norm_now[block] / jnp.sum(p_now * applied, axis=-1, keepdims=True)
            if iteration == 0:
                solved[block] = step * p_now
                correlated[block] = step * reach
            else:
                solved[block] = solved[block] + step * p_now
                correlated[block] = correlated[block] + step * reach
            if iteration < ITERS - 1:
                residual[block] = residual[block] - step * applied
                norm_next = jnp.sum(residual[block] * residual[block], axis=-1, keepdims=True)
                search[block] = residual[block] + norm_next / norm_now[block] * p_now
                norm_now[block] = norm_next
    outputs = []
    for block in range(blocks):
        _, _, g_high, v_high, _, growth = operands[block]
        recall = dot_nt((growth * solved[block]).astype(BF16), g_high)
        outputs.append(recall + dot_nn(correlated[block].astype(BF16), v_high))
    added = dot_nn(jnp.concatenate(outputs, axis=0).astype(BF16), out_weight[...])

    @pl.when(head == 0)
    def _():
        total[...] = added

    @pl.when((head > 0) & (head < pl.num_programs(0) - 1))
    def _():
        total[...] += added

    @pl.when(head == pl.num_programs(0) - 1)
    def _():
        partial_out[...] = (total[...] + added).astype(BF16)


def mixer(projected, taps, prefix, log_gate, regular, out_weight, length):
    rows_total = projected.shape[1]
    heads = regular.shape[0]
    width = heads * DK
    features = out_weight.shape[1]
    share = prefix.shape[0] // heads

    def columns(part):
        return pl.BlockSpec((1, rows_total, DK), lambda head: (part, 0, head))

    return pl.pallas_call(
        mixer_kernel,
        grid=(heads,),
        out_shape=(
            jax.ShapeDtypeStruct((rows_total, features), BF16),
            jax.ShapeDtypeStruct((heads, 2, DK, DK), F32),
            jax.ShapeDtypeStruct((CONV - 1, 3, width), F32),
        ),
        in_specs=[
            pl.BlockSpec(memory_space=pltpu.SMEM),
            columns(0),
            columns(1),
            columns(2),
            pl.BlockSpec((3, CONV, DK), lambda head: (0, 0, head)),
            pl.BlockSpec((share, prefix.shape[1], LANES), lambda head: (head, 0, 0)),
            pl.BlockSpec((1, 1, rows_total), lambda head: (head, 0, 0)),
            pl.BlockSpec((1, 1, DK), lambda head: (head, 0, 0)),
            pl.BlockSpec((DK, features), lambda head: (head, 0)),
        ],
        out_specs=(
            pl.BlockSpec((rows_total, features), lambda head: (0, 0)),
            pl.BlockSpec((1, 2, DK, DK), lambda head: (head, 0, 0, 0)),
            pl.BlockSpec((CONV - 1, 3, DK), lambda head: (0, 0, head)),
        ),
        scratch_shapes=[
            pltpu.VMEM((rows_total + 8, DK), F32),
            pltpu.VMEM((rows_total, features), F32),
        ],
        compiler_params=pltpu.CompilerParams(dimension_semantics=("arbitrary",)),
        name="mixer",
    )(
        length,
        projected,
        projected,
        projected,
        taps,
        prefix,
        log_gate[:, None, :],
        regular[:, None, :],
        out_weight,
    )


def feed_kernel(core, mine, theirs, partial, arrived, gain, gate, up, down, leaving, kept):
    half = mine.shape[1]
    features = 2 * half
    own = pl.multiple_of(core[0] * half, half)
    far = pl.multiple_of((1 - core[0]) * half, half)

    def middle(source, columns, rows):
        added = partial[rows, columns].astype(F32) + arrived[rows, columns].astype(F32)
        return (source[rows, :].astype(F32) + added).astype(BF16).astype(F32)

    step = 256
    for start in range(0, mine.shape[0], step):
        rows = slice(start, start + step)
        middle_own = middle(mine, pl.ds(own, half), rows)
        middle_far = middle(theirs, pl.ds(far, half), rows)
        squares = jnp.sum(
            middle_own * middle_own + middle_far * middle_far, axis=-1, keepdims=True
        )
        inverse = lax.rsqrt(squares * (1.0 / features) + 1e-05)
        normed_own = (middle_own * inverse * gain[:, pl.ds(own, half)]).astype(BF16)
        normed_far = (middle_far * inverse * gain[:, pl.ds(far, half)]).astype(BF16)

        def through(weight):
            return dot_nn(normed_own, weight[pl.ds(own, half), :]) + dot_nn(
                normed_far, weight[pl.ds(far, half), :]
            )

        gated = through(gate)
        hidden = (gated / (1.0 + jnp.exp(-gated)) * through(up)).astype(BF16)
        leaving[rows, :] = dot_nn(hidden, down[:, pl.ds(far, half)]).astype(BF16)
        kept[rows, :] = dot_nn(hidden, down[:, pl.ds(own, half)]) + middle_own


def feed(core, mine, theirs, partial, arrived, gain, gate, up, down):
    vmem = pl.BlockSpec(memory_space=pltpu.VMEM)
    return pl.pallas_call(
        feed_kernel,
        out_shape=(
            jax.ShapeDtypeStruct(mine.shape, BF16),
            jax.ShapeDtypeStruct(mine.shape, F32),
        ),
        in_specs=[pl.BlockSpec(memory_space=pltpu.SMEM)] + [vmem] * 8,
        out_specs=(vmem, vmem),
        name="feed",
    )(core, mine, theirs, partial, arrived, gain, gate, up, down)


def on_device(
    tokens,
    norm_gains,
    qkv_weight,
    conv_weight,
    log_decay,
    regular,
    out_weight,
    gate_up_weight,
    down_weight,
    prefix_cache,
    prefix_tail,
    suffix_len,
    request_group,
    prefix_owner,
):
    rows_total = tokens.shape[0]
    core = lax.axis_index("tensor")
    first = core == 0
    packed = pack(prefix_cache[0], prefix_tail[0], request_group, lax.axis_size("dp"))
    theirs = other_core(tokens)
    arrived = lax.all_to_all(packed, "dp", 0, 0)
    arrived, gate_weight, up_weight = lax.optimization_barrier(
        (arrived, gate_up_weight[:, 0, :], gate_up_weight[:, 1, :])
    )
    prefix = lax.all_to_all(route(prefix_owner, arrived), "dp", 0, 0)
    whole_rows = jnp.concatenate(
        [jnp.where(first, tokens, theirs), jnp.where(first, theirs, tokens)], axis=1
    ).astype(F32)
    normed = rms_rows(whole_rows, norm_gains[0])
    planes = jnp.transpose(qkv_weight, (1, 0, 2))
    projected = jnp.einsum("rd,jdc->jrc", normed, planes, preferred_element_type=F32)
    partial, state_out, tail_out = mixer(
        projected,
        jnp.transpose(conv_weight, (1, 0, 2)),
        prefix,
        log_decay[0],
        regular,
        out_weight,
        suffix_len,
    )
    leaving, kept = feed(
        core.reshape(1).astype(jnp.int32),
        tokens,
        theirs,
        partial,
        other_core(partial),
        norm_gains[1:2],
        gate_weight,
        up_weight,
        down_weight,
    )
    live_rows = jnp.arange(rows_total) < suffix_len[0]
    result = kept + other_core(leaving).astype(F32)
    result = jnp.where(live_rows[:, None], result, 0.0).astype(BF16)
    return (result, state_out[None], tail_out[None])


def solution(mesh):
    return jax.shard_map(
        on_device,
        mesh=mesh,
        in_specs=(
            P("dp", "tensor"),
            P(),
            P(None, None, "tensor"),
            P(None, None, "tensor"),
            P("dp", "tensor", None),
            P("tensor", None),
            P("tensor", None),
            P(None, None, "tensor"),
            P("tensor", None),
            P("dp", "tensor", None, None, None),
            P("dp", None, None, "tensor"),
            P("dp"),
            P("dp"),
            P(),
        ),
        out_specs=(
            P("dp", "tensor"),
            P("dp", "tensor", None, None, None),
            P("dp", None, None, "tensor"),
        ),
        check_vma=False,
    )
```

```python
import functools

import jax
import jax.numpy as jnp
from jax import lax
from jax.experimental import pallas as pl
from jax.experimental.pallas import tpu as pltpu
from jax.sharding import PartitionSpec as P

DK = 128
CONV = 4
BLOCK = 128
ITERS = 4
LANES = 128
BF16 = jnp.bfloat16
F32 = jnp.float32


def rms_rows(floats, gain):
    inverse = lax.rsqrt(jnp.mean(floats * floats, axis=-1, keepdims=True) + 1e-05)
    return (floats * inverse * gain).astype(BF16)


def other_core(array_in):
    return lax.ppermute(array_in, "tensor", [(0, 1), (1, 0)])


def halves(value):
    high = value.astype(BF16)
    return high, (value - high.astype(F32)).astype(BF16)


def dot_nn(left, right):
    return lax.dot_general(left, right, (((1,), (0,)), ((), ())), preferred_element_type=F32)


def dot_nt(left, right):
    return lax.dot_general(left, right, (((1,), (1,)), ((), ())), preferred_element_type=F32)


def dot_tn(left, right):
    return lax.dot_general(left, right, (((0,), (0,)), ((), ())), preferred_element_type=F32)


def pack_kernel(group, cache, tail, packed):
    count, rows, _ = packed.shape
    heads = cache.shape[0]
    share = count // heads
    state_rows = rows - 8
    tail_rows = -(-(CONV - 1) * 3 // share)
    tag = jnp.full((1, LANES), group[0], jnp.int32).astype(F32)
    for head in range(heads):
        lanes = slice(head * DK, (head + 1) * DK)
        for piece in range(share):
            plane, offset = divmod(piece * state_rows, DK)
            parts = [cache[head, plane, offset : offset + state_rows, :]]
            for index in range(piece * tail_rows, (piece + 1) * tail_rows):
                if index < (CONV - 1) * 3:
                    parts.append(tail[index // 3, index % 3, :, lanes])
                else:
                    parts.append(tag)
            parts.append(jnp.broadcast_to(tag, (8 - tail_rows, LANES)))
            packed[head * share + piece] = jnp.concatenate(parts, axis=0).astype(BF16)


def pack(prefix_cache, prefix_tail, request_group, count):
    rows = prefix_cache.shape[0] * 2 * DK // count + 8
    return pl.pallas_call(
        pack_kernel,
        out_shape=jax.ShapeDtypeStruct((count, rows, LANES), BF16),
        in_specs=[
            pl.BlockSpec(memory_space=pltpu.SMEM),
            pl.BlockSpec(memory_space=pltpu.VMEM),
            pl.BlockSpec(memory_space=pltpu.VMEM),
        ],
        out_specs=pl.BlockSpec(memory_space=pltpu.VMEM),
        name="pack",
    )(request_group, prefix_cache, prefix_tail)


def route_kernel(owners, arrived, leaving):
    count, rows, _ = arrived.shape
    groups = owners.shape[0]
    held = [arrived[owners[group]].astype(F32) for group in range(groups)]

    def fill(slot, carry):
        wanted = arrived[slot].astype(F32)[rows - 1 : rows, :]
        chosen = held[0]
        for group in range(1, groups):
            chosen = jnp.where(wanted == float(group), held[group], chosen)
        leaving[slot] = chosen.astype(BF16)
        return carry

    lax.fori_loop(0, count, fill, 0)


def route(prefix_owner, arrived):
    return pl.pallas_call(
        route_kernel,
        out_shape=jax.ShapeDtypeStruct(arrived.shape, arrived.dtype),
        in_specs=[
            pl.BlockSpec(memory_space=pltpu.SMEM),
            pl.BlockSpec(memory_space=pltpu.VMEM),
        ],
        out_specs=pl.BlockSpec(memory_space=pltpu.VMEM),
        name="route",
    )(prefix_owner, arrived)


def mixer_kernel(
    length_ref,
    query_in,
    key_in,
    value_in,
    taps,
    prefix,
    decay,
    regular,
    out_weight,
    partial_out,
    state_out,
    tail_out,
    extended,
    total,
):
    rows_total = query_in.shape[1]
    blocks = rows_total // BLOCK
    head = pl.program_id(0)
    length = length_ref[0]
    share, chunk_rows, _ = prefix.shape
    state_rows = chunk_rows - 8
    tail_rows = -(-(CONV - 1) * 3 // share)
    chunks = [prefix[piece].astype(F32) for piece in range(share)]
    state = jnp.concatenate([chunk[:state_rows] for chunk in chunks], axis=0)
    hstate, gstate = state[:DK], state[DK:]

    live = lax.broadcasted_iota(jnp.int32, (rows_total, 1), 0) < length
    activated = []
    for part, source in enumerate((query_in, key_in, value_in)):
        for before in range(CONV - 1):
            piece, inside = divmod(before * 3 + part, tail_rows)
            place = state_rows + inside
            extended[5 + before : 6 + before, :] = chunks[piece][place : place + 1]
        extended[8 : 8 + rows_total, :] = source[0]
        convolved = taps[part, 0:1, :] * extended[pl.ds(5, rows_total), :]
        for tap in range(1, CONV):
            convolved = (
                convolved + taps[part, tap : tap + 1, :] * extended[pl.ds(5 + tap, rows_total), :]
            )
        for place in range(CONV - 1):
            tail_out[place, part] = extended[pl.ds(length + 5 + place, 1), :]
        activated.append(convolved / (1.0 + jnp.exp(-convolved)))
    queries, key_rows, value_rows = activated
    queries = queries * lax.rsqrt(jnp.sum(queries * queries, axis=-1, keepdims=True) + 1e-06)
    key_rows = key_rows * lax.rsqrt(jnp.sum(key_rows * key_rows, axis=-1, keepdims=True) + 1e-06)
    key_rows = jnp.where(live, key_rows, 0.0)
    value_rows = jnp.where(live, value_rows, 0.0)

    lane = lax.broadcasted_iota(jnp.int32, (BLOCK, BLOCK), 1)
    row = lax.broadcasted_iota(jnp.int32, (BLOCK, BLOCK), 0)
    causal = row >= lane
    regular_row = regular[0]

    operands = []
    for block in range(blocks):
        rows = slice(block * BLOCK, (block + 1) * BLOCK)
        keys, values = key_rows[rows], value_rows[rows]
        gates = decay[0, :, block * BLOCK : (block + 1) * BLOCK]
        position = lax.broadcasted_iota(jnp.int32, (1, BLOCK), 1) + block * BLOCK
        gates = jnp.where(position < length, gates, 0.0)
        down = jnp.sum(jnp.where(causal, gates, 0.0), axis=1, keepdims=True)
        wide = jnp.broadcast_to(down, (BLOCK, BLOCK))
        differ = wide - wide.T
        weights = jnp.where(causal, jnp.exp(jnp.minimum(differ, 0.0)), 0.0)
        growth = jnp.exp(down)
        last = down[BLOCK - 1 : BLOCK, :]
        root_tail = jnp.exp(0.5 * (last - down))
        decay_last = jnp.exp(last)
        keys_high = keys.astype(BF16)
        operands.append(
            (
                keys_high,
                jnp.concatenate([hstate.astype(BF16), keys_high], axis=0),
                gstate.astype(BF16),
                values.astype(BF16),
                weights,
                growth,
            )
        )
        grown = jnp.concatenate([keys * root_tail, values * root_tail], axis=1).astype(BF16)
        update = dot_tn(grown, grown[:, :DK])
        hstate = decay_last * hstate + update[:DK]
        gstate = decay_last * gstate + update[DK:]
    state_out[0, 0] = hstate
    state_out[0, 1] = gstate

    search = [queries[block * BLOCK : (block + 1) * BLOCK] for block in range(blocks)]
    residual = list(search)
    solved = [None] * blocks
    correlated = [None] * blocks
    norm_now = [jnp.sum(r * r, axis=-1, keepdims=True) for r in residual]
    for iteration in range(ITERS):
        for block in range(blocks):
            k_high, mix_high, _, _, weights, growth = operands[block]
            p_now = search[block]
            p_high, p_low = halves(p_now)
            reach = (dot_nt(p_high, k_high) + dot_nt(p_low, k_high)) * weights
            b_high, b_low = halves(jnp.concatenate([growth * p_now, reach], axis=1))
            applied = dot_nn(b_high, mix_high) + dot_nn(b_low, mix_high) + regular_row * p_now
            step = norm_now[block] / jnp.sum(p_now * applied, axis=-1, keepdims=True)
            if iteration == 0:
                solved[block] = step * p_now
                correlated[block] = step * reach
            else:
                solved[block] = solved[block] + step * p_now
                correlated[block] = correlated[block] + step * reach
            if iteration < ITERS - 1:
                residual[block] = residual[block] - step * applied
                norm_next = jnp.sum(residual[block] * residual[block], axis=-1, keepdims=True)
                search[block] = residual[block] + norm_next / norm_now[block] * p_now
                norm_now[block] = norm_next
    outputs = []
    for block in range(blocks):
        _, _, g_high, v_high, _, growth = operands[block]
        recall = dot_nt((growth * solved[block]).astype(BF16), g_high)
        outputs.append(recall + dot_nn(correlated[block].astype(BF16), v_high))
    added = dot_nn(jnp.concatenate(outputs, axis=0).astype(BF16), out_weight[...])

    @pl.when(head == 0)
    def _():
        total[...] = added

    @pl.when((head > 0) & (head < pl.num_programs(0) - 1))
    def _():
        total[...] += added

    @pl.when(head == pl.num_programs(0) - 1)
    def _():
        partial_out[...] = (total[...] + added).astype(BF16)


def mixer(projected, taps, prefix, log_gate, regular, out_weight, length):
    rows_total = projected.shape[1]
    heads = regular.shape[0]
    width = heads * DK
    features = out_weight.shape[1]
    share = prefix.shape[0] // heads

    def columns(part):
        return pl.BlockSpec((1, rows_total, DK), lambda head: (part, 0, head))

    return pl.pallas_call(
        mixer_kernel,
        grid=(heads,),
        out_shape=(
            jax.ShapeDtypeStruct((rows_total, features), BF16),
            jax.ShapeDtypeStruct((heads, 2, DK, DK), F32),
            jax.ShapeDtypeStruct((CONV - 1, 3, 1, width), F32),
        ),
        in_specs=[
            pl.BlockSpec(memory_space=pltpu.SMEM),
            columns(0),
            columns(1),
            columns(2),
            pl.BlockSpec((3, CONV, DK), lambda head: (0, 0, head)),
            pl.BlockSpec((share, prefix.shape[1], LANES), lambda head: (head, 0, 0)),
            pl.BlockSpec((1, 1, rows_total), lambda head: (head, 0, 0)),
            pl.BlockSpec((1, 1, DK), lambda head: (head, 0, 0)),
            pl.BlockSpec((DK, features), lambda head: (head, 0)),
        ],
        out_specs=(
            pl.BlockSpec((rows_total, features), lambda head: (0, 0)),
            pl.BlockSpec((1, 2, DK, DK), lambda head: (head, 0, 0, 0)),
            pl.BlockSpec((CONV - 1, 3, 1, DK), lambda head: (0, 0, 0, head)),
        ),
        scratch_shapes=[
            pltpu.VMEM((rows_total + 8, DK), F32),
            pltpu.VMEM((rows_total, features), F32),
        ],
        compiler_params=pltpu.CompilerParams(dimension_semantics=("arbitrary",)),
        name="mixer",
    )(
        length,
        projected,
        projected,
        projected,
        taps,
        prefix,
        log_gate[:, None, :],
        regular[:, None, :],
        out_weight,
    )


def on_device(
    tokens,
    norm_gains,
    qkv_weight,
    conv_weight,
    log_decay,
    regular,
    out_weight,
    gate_up_weight,
    down_weight,
    prefix_cache,
    prefix_tail,
    suffix_len,
    request_group,
    prefix_owner,
):
    rows_total, half = tokens.shape
    first = lax.axis_index("tensor") == 0
    packed = pack(
        prefix_cache[0],
        jnp.transpose(prefix_tail, (1, 2, 0, 3)),
        request_group,
        lax.axis_size("dp"),
    )
    theirs = other_core(tokens)
    arrived = lax.all_to_all(packed, "dp", 0, 0)
    whole_rows = jnp.concatenate(
        [jnp.where(first, tokens, theirs), jnp.where(first, theirs, tokens)], axis=1
    ).astype(F32)
    normed = rms_rows(whole_rows, norm_gains[0])
    planes = jnp.transpose(qkv_weight, (1, 0, 2))
    projected = jnp.einsum("rd,jdc->jrc", normed, planes, preferred_element_type=F32)
    arrived, projected, gate_up_weight = lax.optimization_barrier(
        (arrived, projected, gate_up_weight)
    )
    prefix = lax.all_to_all(route(prefix_owner, arrived), "dp", 0, 0)
    prefix, gate_up_matrix = lax.optimization_barrier(
        (prefix, gate_up_weight.reshape(gate_up_weight.shape[0], -1))
    )
    partial, state_out, tail_out = mixer(
        projected,
        jnp.transpose(conv_weight, (1, 0, 2)),
        prefix,
        log_decay[0],
        regular,
        out_weight,
        suffix_len,
    )
    attended = partial.astype(F32) + other_core(partial).astype(F32)
    middle = (whole_rows + attended).astype(BF16)
    gate_up = jnp.dot(
        rms_rows(middle.astype(F32), norm_gains[1]), gate_up_matrix, preferred_element_type=F32
    )
    hidden_width = gate_up.shape[1] // 2
    hidden = (jax.nn.silu(gate_up[:, :hidden_width]) * gate_up[:, hidden_width:]).astype(BF16)
    forward = jnp.dot(hidden, down_weight, preferred_element_type=F32)
    left, right = forward[:, :half], forward[:, half:]
    leaving = other_core(jnp.where(first, right, left).astype(BF16))
    kept = jnp.where(first, left, right) + leaving.astype(F32)
    base = jnp.where(first, middle[:, :half], middle[:, half:]).astype(F32)
    live_rows = jnp.arange(rows_total) < suffix_len[0]
    result = jnp.where(live_rows[:, None], base + kept, 0.0).astype(BF16)
    return (result, state_out[None], jnp.transpose(tail_out, (2, 0, 1, 3)))


def solution(mesh):
    return jax.shard_map(
        on_device,
        mesh=mesh,
        in_specs=(
            P("dp", "tensor"),
            P(),
            P(None, None, "tensor"),
            P(None, None, "tensor"),
            P("dp", "tensor", None),
            P("tensor", None),
            P("tensor", None),
            P(None, None, "tensor"),
            P("tensor", None),
            P("dp", "tensor", None, None, None),
            P("dp", None, None, "tensor"),
            P("dp"),
            P("dp"),
            P(),
        ),
        out_specs=(
            P("dp", "tensor"),
            P("dp", "tensor", None, None, None),
            P("dp", None, None, "tensor"),
        ),
        check_vma=False,
    )
```

```python
import functools

import jax
import jax.numpy as jnp
from jax import lax
from jax.experimental import pallas as pl
from jax.experimental.pallas import tpu as pltpu
from jax.sharding import PartitionSpec as P

DK = 128
CONV = 4
BLOCK = 128
ITERS = 4
LANES = 128
BF16 = jnp.bfloat16
F32 = jnp.float32


def rms_rows(floats, gain):
    inverse = lax.rsqrt(jnp.mean(floats * floats, axis=-1, keepdims=True) + 1e-05)
    return (floats * inverse * gain).astype(BF16)


def other_core(array_in):
    return lax.ppermute(array_in, "tensor", [(0, 1), (1, 0)])


def halves(value):
    high = value.astype(BF16)
    return high, (value - high.astype(F32)).astype(BF16)


def dot_nn(left, right):
    return lax.dot_general(left, right, (((1,), (0,)), ((), ())), preferred_element_type=F32)


def dot_nt(left, right):
    return lax.dot_general(left, right, (((1,), (1,)), ((), ())), preferred_element_type=F32)


def dot_tn(left, right):
    return lax.dot_general(left, right, (((0,), (0,)), ((), ())), preferred_element_type=F32)


def pack_kernel(group, cache, tail, packed):
    count, rows, _ = packed.shape
    heads = cache.shape[0]
    share = count // heads
    state_rows = rows - 8
    tail_rows = -(-(CONV - 1) * 3 // share)
    tag = jnp.full((1, LANES), group[0], jnp.int32).astype(F32)
    for head in range(heads):
        lanes = slice(head * DK, (head + 1) * DK)
        for piece in range(share):
            plane, offset = divmod(piece * state_rows, DK)
            parts = [cache[head, plane, offset : offset + state_rows, :]]
            for index in range(piece * tail_rows, (piece + 1) * tail_rows):
                if index < (CONV - 1) * 3:
                    parts.append(tail[index // 3, index % 3, :, lanes])
                else:
                    parts.append(tag)
            parts.append(jnp.broadcast_to(tag, (8 - tail_rows, LANES)))
            packed[head * share + piece] = jnp.concatenate(parts, axis=0).astype(BF16)


def pack(prefix_cache, prefix_tail, request_group, count):
    rows = prefix_cache.shape[0] * 2 * DK // count + 8
    return pl.pallas_call(
        pack_kernel,
        out_shape=jax.ShapeDtypeStruct((count, rows, LANES), BF16),
        in_specs=[
            pl.BlockSpec(memory_space=pltpu.SMEM),
            pl.BlockSpec(memory_space=pltpu.VMEM),
            pl.BlockSpec(memory_space=pltpu.VMEM),
        ],
        out_specs=pl.BlockSpec(memory_space=pltpu.VMEM),
        name="pack",
    )(request_group, prefix_cache, prefix_tail)


def route_kernel(owners, arrived, leaving):
    count, rows, _ = arrived.shape
    groups = owners.shape[0]
    held = [arrived[owners[group]].astype(F32) for group in range(groups)]

    def fill(slot, carry):
        wanted = arrived[slot].astype(F32)[rows - 1 : rows, :]
        chosen = held[0]
        for group in range(1, groups):
            chosen = jnp.where(wanted == float(group), held[group], chosen)
        leaving[slot] = chosen.astype(BF16)
        return carry

    lax.fori_loop(0, count, fill, 0)


def route(prefix_owner, arrived):
    return pl.pallas_call(
        route_kernel,
        out_shape=jax.ShapeDtypeStruct(arrived.shape, arrived.dtype),
        in_specs=[
            pl.BlockSpec(memory_space=pltpu.SMEM),
            pl.BlockSpec(memory_space=pltpu.VMEM),
        ],
        out_specs=pl.BlockSpec(memory_space=pltpu.VMEM),
        name="route",
    )(prefix_owner, arrived)


def mixer_kernel(
    length_ref,
    query_in,
    key_in,
    value_in,
    taps,
    prefix,
    decay,
    regular,
    out_weight,
    partial_out,
    state_out,
    tail_out,
    extended,
    total,
):
    rows_total = query_in.shape[1]
    blocks = rows_total // BLOCK
    step_id = pl.program_id(0)
    length = length_ref[0]
    local_heads = regular.shape[0]
    share = prefix.shape[0] // local_heads
    state_rows = prefix.shape[1] - 8
    tail_rows = -(-(CONV - 1) * 3 // share)
    live = lax.broadcasted_iota(jnp.int32, (rows_total, 1), 0) < length
    lane = lax.broadcasted_iota(jnp.int32, (BLOCK, BLOCK), 1)
    row = lax.broadcasted_iota(jnp.int32, (BLOCK, BLOCK), 0)
    causal = row >= lane

    chains = []
    for local in range(local_heads):
        lanes = slice(local * DK, (local + 1) * DK)
        chunks = [prefix[local * share + piece].astype(F32) for piece in range(share)]
        state = jnp.concatenate([chunk[:state_rows] for chunk in chunks], axis=0)
        hstate, gstate = state[:DK], state[DK:]
        activated = []
        for part, source in enumerate((query_in, key_in, value_in)):
            longer = extended.at[local * 3 + part]
            for before in range(CONV - 1):
                piece, inside = divmod(before * 3 + part, tail_rows)
                place = state_rows + inside
                longer[5 + before : 6 + before, :] = chunks[piece][place : place + 1]
            longer[8 : 8 + rows_total, :] = source[0, :, lanes]
            convolved = taps[part, 0:1, lanes] * longer[pl.ds(5, rows_total), :]
            for tap in range(1, CONV):
                convolved = (
                    convolved
                    + taps[part, tap : tap + 1, lanes] * longer[pl.ds(5 + tap, rows_total), :]
                )
            for place in range(CONV - 1):
                tail_out[place, part, :, lanes] = longer[pl.ds(length + 5 + place, 1), :]
            activated.append(convolved / (1.0 + jnp.exp(-convolved)))
        queries, key_rows, value_rows = activated
        queries = queries * lax.rsqrt(jnp.sum(queries * queries, axis=-1, keepdims=True) + 1e-06)
        key_rows = key_rows * lax.rsqrt(
            jnp.sum(key_rows * key_rows, axis=-1, keepdims=True) + 1e-06
        )
        key_rows = jnp.where(live, key_rows, 0.0)
        value_rows = jnp.where(live, value_rows, 0.0)
        for block in range(blocks):
            rows = slice(block * BLOCK, (block + 1) * BLOCK)
            keys, values = key_rows[rows], value_rows[rows]
            gates = decay[local, :, block * BLOCK : (block + 1) * BLOCK]
            position = lax.broadcasted_iota(jnp.int32, (1, BLOCK), 1) + block * BLOCK
            gates = jnp.where(position < length, gates, 0.0)
            down = jnp.sum(jnp.where(causal, gates, 0.0), axis=1, keepdims=True)
            wide = jnp.broadcast_to(down, (BLOCK, BLOCK))
            differ = wide - wide.T
            weights = jnp.where(causal, jnp.exp(jnp.minimum(differ, 0.0)), 0.0)
            growth = jnp.exp(wide)
            last = down[BLOCK - 1 : BLOCK, :]
            root_tail = jnp.exp(0.5 * (last - down))
            decay_last = jnp.exp(last)
            chains.append(
                (
                    queries[rows],
                    keys.astype(BF16),
                    jnp.concatenate([keys.T, hstate], axis=1).astype(BF16),
                    gstate.astype(BF16),
                    values.astype(BF16),
                    weights,
                    growth,
                    regular[local],
                )
            )
            grown = jnp.concatenate([keys * root_tail, values * root_tail], axis=1).astype(BF16)
            update = dot_tn(grown, grown[:, :DK])
            hstate = decay_last * hstate + update[:DK]
            gstate = decay_last * gstate + update[DK:]
        state_out[local, 0] = hstate
        state_out[local, 1] = gstate

    count = len(chains)
    search = [chain[0] for chain in chains]
    residual = list(search)
    norm_now = [jnp.sum(r * r, axis=-1, keepdims=True) for r in residual]
    everyone = range(count)
    for iteration in range(ITERS):
        both = [
            dot_nn(jnp.concatenate(halves(search[index]), axis=0), chains[index][2])
            for index in everyone
        ]
        both = [pair[:BLOCK] + pair[BLOCK:] for pair in both]
        reach = [both[index][:, :BLOCK] * chains[index][5] for index in everyone]
        near = [
            dot_nn(jnp.concatenate(halves(reach[index]), axis=0), chains[index][1])
            for index in everyone
        ]
        applied = [
            chains[index][6] * both[index][:, BLOCK:]
            + (near[index][:BLOCK] + near[index][BLOCK:])
            + chains[index][7] * search[index]
            for index in everyone
        ]
        step = [
            norm_now[index] / jnp.sum(search[index] * applied[index], axis=-1, keepdims=True)
            for index in everyone
        ]
        if iteration == 0:
            solved = [step[index] * search[index] for index in everyone]
            correlated = [step[index] * reach[index] for index in everyone]
        else:
            solved = [solved[index] + step[index] * search[index] for index in everyone]
            correlated = [correlated[index] + step[index] * reach[index] for index in everyone]
        if iteration < ITERS - 1:
            residual = [residual[index] - step[index] * applied[index] for index in everyone]
            norm_next = [jnp.sum(r * r, axis=-1, keepdims=True) for r in residual]
            search = [
                residual[index] + norm_next[index] / norm_now[index] * search[index]
                for index in everyone
            ]
            norm_now = norm_next
    outputs = []
    for index in range(count):
        _, _, _, g_high, v_high, _, growth, _ = chains[index]
        recall = dot_nt((growth * solved[index]).astype(BF16), g_high)
        outputs.append((recall + dot_nn(correlated[index].astype(BF16), v_high)).astype(BF16))
    heads_out = jnp.concatenate(
        [
            jnp.concatenate(outputs[local * blocks : (local + 1) * blocks], axis=0)
            for local in range(local_heads)
        ],
        axis=1,
    )
    added = dot_nn(heads_out, out_weight[...])
    steps = pl.num_programs(0)

    @pl.when(step_id == 0)
    def _():
        total[...] = added

    @pl.when((step_id > 0) & (step_id < steps - 1))
    def _():
        total[...] += added

    @pl.when(step_id == steps - 1)
    def _():
        partial_out[...] = (total[...] + added).astype(BF16)


def mixer(projected, taps, prefix, log_gate, regular, out_weight, length):
    rows_total = projected.shape[1]
    heads = regular.shape[0]
    together = 2
    width = heads * DK
    features = out_weight.shape[1]
    share = prefix.shape[0] // heads

    def columns(part):
        return pl.BlockSpec((1, rows_total, together * DK), lambda step: (part, 0, step))

    return pl.pallas_call(
        mixer_kernel,
        grid=(heads // together,),
        out_shape=(
            jax.ShapeDtypeStruct((rows_total, features), BF16),
            jax.ShapeDtypeStruct((heads, 2, DK, DK), F32),
            jax.ShapeDtypeStruct((CONV - 1, 3, 1, width), F32),
        ),
        in_specs=[
            pl.BlockSpec(memory_space=pltpu.SMEM),
            columns(0),
            columns(1),
            columns(2),
            pl.BlockSpec((3, CONV, together * DK), lambda step: (0, 0, step)),
            pl.BlockSpec((together * share, prefix.shape[1], LANES), lambda step: (step, 0, 0)),
            pl.BlockSpec((together, 1, rows_total), lambda step: (step, 0, 0)),
            pl.BlockSpec((together, 1, DK), lambda step: (step, 0, 0)),
            pl.BlockSpec((together * DK, features), lambda step: (step, 0)),
        ],
        out_specs=(
            pl.BlockSpec((rows_total, features), lambda step: (0, 0)),
            pl.BlockSpec((together, 2, DK, DK), lambda step: (step, 0, 0, 0)),
            pl.BlockSpec((CONV - 1, 3, 1, together * DK), lambda step: (0, 0, 0, step)),
        ),
        scratch_shapes=[
            pltpu.VMEM((together * 3, rows_total + 8, DK), F32),
            pltpu.VMEM((rows_total, features), F32),
        ],
        compiler_params=pltpu.CompilerParams(dimension_semantics=("arbitrary",)),
        name="mixer",
    )(
        length,
        projected,
        projected,
        projected,
        taps,
        prefix,
        log_gate[:, None, :],
        regular[:, None, :],
        out_weight,
    )


def on_device(
    tokens,
    norm_gains,
    qkv_weight,
    conv_weight,
    log_decay,
    regular,
    out_weight,
    gate_up_weight,
    down_weight,
    prefix_cache,
    prefix_tail,
    suffix_len,
    request_group,
    prefix_owner,
):
    rows_total, half = tokens.shape
    first = lax.axis_index("tensor") == 0
    packed = pack(
        prefix_cache[0],
        jnp.transpose(prefix_tail, (1, 2, 0, 3)),
        request_group,
        lax.axis_size("dp"),
    )
    packed, tokens = lax.optimization_barrier((packed, tokens))
    theirs = other_core(tokens)
    arrived = lax.all_to_all(packed, "dp", 0, 0)
    whole_rows = jnp.concatenate(
        [jnp.where(first, tokens, theirs), jnp.where(first, theirs, tokens)], axis=1
    ).astype(F32)
    normed = rms_rows(whole_rows, norm_gains[0])
    planes = jnp.transpose(qkv_weight, (1, 0, 2))
    projected = jnp.einsum("rd,jdc->jrc", normed, planes, preferred_element_type=F32)
    arrived, projected, gate_up_weight = lax.optimization_barrier(
        (arrived, projected, gate_up_weight)
    )
    prefix = lax.all_to_all(route(prefix_owner, arrived), "dp", 0, 0)
    prefix, gate_up_matrix = lax.optimization_barrier(
        (prefix, gate_up_weight.reshape(gate_up_weight.shape[0], -1))
    )
    partial, state_out, tail_out = mixer(
        projected,
        jnp.transpose(conv_weight, (1, 0, 2)),
        prefix,
        log_decay[0],
        regular,
        out_weight,
        suffix_len,
    )
    attended = partial.astype(F32) + other_core(partial).astype(F32)
    middle = (whole_rows + attended).astype(BF16)
    gate_up = jnp.dot(
        rms_rows(middle.astype(F32), norm_gains[1]), gate_up_matrix, preferred_element_type=F32
    )
    hidden_width = gate_up.shape[1] // 2
    hidden = (jax.nn.silu(gate_up[:, :hidden_width]) * gate_up[:, hidden_width:]).astype(BF16)
    forward = jnp.dot(hidden, down_weight, preferred_element_type=F32)
    left, right = forward[:, :half], forward[:, half:]
    leaving = other_core(jnp.where(first, right, left).astype(BF16))
    kept = jnp.where(first, left, right) + leaving.astype(F32)
    base = jnp.where(first, middle[:, :half], middle[:, half:]).astype(F32)
    live_rows = jnp.arange(rows_total) < suffix_len[0]
    result = jnp.where(live_rows[:, None], base + kept, 0.0).astype(BF16)
    return (result, state_out[None], jnp.transpose(tail_out, (2, 0, 1, 3)))


def solution(mesh):
    return jax.shard_map(
        on_device,
        mesh=mesh,
        in_specs=(
            P("dp", "tensor"),
            P(),
            P(None, None, "tensor"),
            P(None, None, "tensor"),
            P("dp", "tensor", None),
            P("tensor", None),
            P("tensor", None),
            P(None, None, "tensor"),
            P("tensor", None),
            P("dp", "tensor", None, None, None),
            P("dp", None, None, "tensor"),
            P("dp"),
            P("dp"),
            P(),
        ),
        out_specs=(
            P("dp", "tensor"),
            P("dp", "tensor", None, None, None),
            P("dp", None, None, "tensor"),
        ),
        check_vma=False,
    )
```

```python
import functools

import jax
import jax.numpy as jnp
from jax import lax
from jax.experimental import pallas as pl
from jax.experimental.pallas import tpu as pltpu
from jax.sharding import PartitionSpec as P

DK = 128
CONV = 4
BLOCK = 128
ITERS = 4
LANES = 128
BF16 = jnp.bfloat16
F32 = jnp.float32


def rms_rows(floats, gain):
    inverse = lax.rsqrt(jnp.mean(floats * floats, axis=-1, keepdims=True) + 1e-05)
    return (floats * inverse * gain).astype(BF16)


def other_core(array_in):
    return lax.ppermute(array_in, "tensor", [(0, 1), (1, 0)])


def halves(value):
    high = value.astype(BF16)
    return high, (value - high.astype(F32)).astype(BF16)


def dot_nn(left, right):
    return lax.dot_general(left, right, (((1,), (0,)), ((), ())), preferred_element_type=F32)


def dot_nt(left, right):
    return lax.dot_general(left, right, (((1,), (1,)), ((), ())), preferred_element_type=F32)


def dot_tn(left, right):
    return lax.dot_general(left, right, (((0,), (0,)), ((), ())), preferred_element_type=F32)


def pack_kernel(group, cache, tail, packed):
    count, rows, _ = packed.shape
    heads = cache.shape[0]
    share = count // heads
    state_rows = rows - 8
    tail_rows = -(-(CONV - 1) * 3 // share)
    tag = jnp.full((1, LANES), group[0], jnp.int32).astype(F32)
    for head in range(heads):
        lanes = slice(head * DK, (head + 1) * DK)
        for piece in range(share):
            plane, offset = divmod(piece * state_rows, DK)
            parts = [cache[head, plane, offset : offset + state_rows, :]]
            for index in range(piece * tail_rows, (piece + 1) * tail_rows):
                if index < (CONV - 1) * 3:
                    parts.append(tail[index // 3, index % 3, :, lanes])
                else:
                    parts.append(tag)
            parts.append(jnp.broadcast_to(tag, (8 - tail_rows, LANES)))
            packed[head * share + piece] = jnp.concatenate(parts, axis=0).astype(BF16)


def pack(prefix_cache, prefix_tail, request_group, count):
    rows = prefix_cache.shape[0] * 2 * DK // count + 8
    return pl.pallas_call(
        pack_kernel,
        out_shape=jax.ShapeDtypeStruct((count, rows, LANES), BF16),
        in_specs=[
            pl.BlockSpec(memory_space=pltpu.SMEM),
            pl.BlockSpec(memory_space=pltpu.VMEM),
            pl.BlockSpec(memory_space=pltpu.VMEM),
        ],
        out_specs=pl.BlockSpec(memory_space=pltpu.VMEM),
        name="pack",
    )(request_group, prefix_cache, prefix_tail)


def route_kernel(owners, source, target, arrived, leaving):
    pltpu.sync_copy(source, arrived)
    count, rows, _ = arrived.shape
    groups = owners.shape[0]
    held = [arrived[owners[group]].astype(F32) for group in range(groups)]

    def fill(slot, carry):
        wanted = arrived[slot].astype(F32)[rows - 1 : rows, :]
        chosen = held[0]
        for group in range(1, groups):
            chosen = jnp.where(wanted == float(group), held[group], chosen)
        leaving[slot] = chosen.astype(BF16)
        return carry

    lax.fori_loop(0, count, fill, 0)
    pltpu.sync_copy(leaving, target)


def route(prefix_owner, arrived):
    return pl.pallas_call(
        route_kernel,
        out_shape=pltpu.HBM(arrived.shape, arrived.dtype),
        in_specs=[
            pl.BlockSpec(memory_space=pltpu.SMEM),
            pl.BlockSpec(memory_space=pl.ANY),
        ],
        out_specs=pl.BlockSpec(memory_space=pltpu.HBM),
        scratch_shapes=[pltpu.VMEM(arrived.shape, arrived.dtype)] * 2,
        compiler_params=pltpu.CompilerParams(vmem_limit_bytes=8 << 20),
        name="route",
    )(prefix_owner, arrived)


def mixer_kernel(
    heads_total,
    upper_rows,
    length_ref,
    query_in,
    key_in,
    value_in,
    taps,
    prefix_source,
    decay,
    regular,
    out_weight,
    upper_out,
    lower_out,
    state_out,
    tail_out,
    extended,
    total,
    prefix,
):
    rows_total = query_in.shape[1]
    blocks = rows_total // BLOCK
    step_id = pl.program_id(0)
    length = length_ref[0]
    local_heads = regular.shape[0]
    steps = pl.num_programs(0)
    share = prefix_source.shape[0] // heads_total

    @pl.when(step_id == 0)
    def _():
        pltpu.sync_copy(prefix_source, prefix)

    state_rows = prefix.shape[1] - 8
    tail_rows = -(-(CONV - 1) * 3 // share)
    live = lax.broadcasted_iota(jnp.int32, (rows_total, 1), 0) < length
    lane = lax.broadcasted_iota(jnp.int32, (BLOCK, BLOCK), 1)
    row = lax.broadcasted_iota(jnp.int32, (BLOCK, BLOCK), 0)
    causal = row >= lane

    chains = []
    for local in range(local_heads):
        lanes = slice(local * DK, (local + 1) * DK)
        chunks = [
            prefix[(step_id * local_heads + local) * share + piece].astype(F32)
            for piece in range(share)
        ]
        state = jnp.concatenate([chunk[:state_rows] for chunk in chunks], axis=0)
        hstate, gstate = state[:DK], state[DK:]
        activated = []
        for part, source in enumerate((query_in, key_in, value_in)):
            longer = extended.at[local * 3 + part]
            for before in range(CONV - 1):
                piece, inside = divmod(before * 3 + part, tail_rows)
                place = state_rows + inside
                longer[5 + before : 6 + before, :] = chunks[piece][place : place + 1]
            longer[8 : 8 + rows_total, :] = source[0, :, lanes]
            convolved = taps[part, 0:1, lanes] * longer[pl.ds(5, rows_total), :]
            for tap in range(1, CONV):
                convolved = (
                    convolved
                    + taps[part, tap : tap + 1, lanes] * longer[pl.ds(5 + tap, rows_total), :]
                )
            for place in range(CONV - 1):
                tail_out[place, part, :, lanes] = longer[pl.ds(length + 5 + place, 1), :]
            activated.append(convolved / (1.0 + jnp.exp(-convolved)))
        queries, key_rows, value_rows = activated
        queries = queries * lax.rsqrt(jnp.sum(queries * queries, axis=-1, keepdims=True) + 1e-06)
        key_rows = key_rows * lax.rsqrt(
            jnp.sum(key_rows * key_rows, axis=-1, keepdims=True) + 1e-06
        )
        key_rows = jnp.where(live, key_rows, 0.0)
        value_rows = jnp.where(live, value_rows, 0.0)
        for block in range(blocks):
            rows = slice(block * BLOCK, (block + 1) * BLOCK)
            keys, values = key_rows[rows], value_rows[rows]
            gates = decay[local, :, block * BLOCK : (block + 1) * BLOCK]
            position = lax.broadcasted_iota(jnp.int32, (1, BLOCK), 1) + block * BLOCK
            gates = jnp.where(position < length, gates, 0.0)
            down = jnp.sum(jnp.where(causal, gates, 0.0), axis=1, keepdims=True)
            wide = jnp.broadcast_to(down, (BLOCK, BLOCK))
            differ = wide - wide.T
            weights = jnp.where(causal, jnp.exp(jnp.minimum(differ, 0.0)), 0.0)
            growth = jnp.exp(wide)
            last = down[BLOCK - 1 : BLOCK, :]
            root_tail = jnp.exp(0.5 * (last - down))
            decay_last = jnp.exp(last)
            chains.append(
                (
                    queries[rows],
                    keys.astype(BF16),
                    jnp.concatenate([keys.T, hstate], axis=1).astype(BF16),
                    gstate.astype(BF16),
                    values.astype(BF16),
                    weights,
                    growth,
                    regular[local],
                )
            )
            grown = jnp.concatenate([keys * root_tail, values * root_tail], axis=1).astype(BF16)
            update = dot_tn(grown, grown[:, :DK])
            hstate = decay_last * hstate + update[:DK]
            gstate = decay_last * gstate + update[DK:]
        state_out[local, 0] = hstate
        state_out[local, 1] = gstate

    count = len(chains)
    search = [chain[0] for chain in chains]
    residual = list(search)
    norm_now = [jnp.sum(r * r, axis=-1, keepdims=True) for r in residual]
    everyone = range(count)
    for iteration in range(ITERS):
        both = [
            dot_nn(jnp.concatenate(halves(search[index]), axis=0), chains[index][2])
            for index in everyone
        ]
        both = [pair[:BLOCK] + pair[BLOCK:] for pair in both]
        reach = [both[index][:, :BLOCK] * chains[index][5] for index in everyone]
        near = [
            dot_nn(jnp.concatenate(halves(reach[index]), axis=0), chains[index][1])
            for index in everyone
        ]
        applied = [
            chains[index][6] * both[index][:, BLOCK:]
            + (near[index][:BLOCK] + near[index][BLOCK:])
            + chains[index][7] * search[index]
            for index in everyone
        ]
        step = [
            norm_now[index] / jnp.sum(search[index] * applied[index], axis=-1, keepdims=True)
            for index in everyone
        ]
        if iteration == 0:
            solved = [step[index] * search[index] for index in everyone]
            correlated = [step[index] * reach[index] for index in everyone]
        else:
            solved = [solved[index] + step[index] * search[index] for index in everyone]
            correlated = [correlated[index] + step[index] * reach[index] for index in everyone]
        if iteration < ITERS - 1:
            residual = [residual[index] - step[index] * applied[index] for index in everyone]
            norm_next = [jnp.sum(r * r, axis=-1, keepdims=True) for r in residual]
            search = [
                residual[index] + norm_next[index] / norm_now[index] * search[index]
                for index in everyone
            ]
            norm_now = norm_next
    outputs = []
    for index in range(count):
        _, _, _, g_high, v_high, _, growth, _ = chains[index]
        recall = dot_nt((growth * solved[index]).astype(BF16), g_high)
        outputs.append((recall + dot_nn(correlated[index].astype(BF16), v_high)).astype(BF16))
    heads_out = jnp.concatenate(
        [
            jnp.concatenate(outputs[local * blocks : (local + 1) * blocks], axis=0)
            for local in range(local_heads)
        ],
        axis=1,
    )
    added = dot_nn(heads_out, out_weight[...])

    @pl.when(step_id == 0)
    def _():
        total[...] = added

    @pl.when((step_id > 0) & (step_id < steps - 1))
    def _():
        total[...] += added

    @pl.when(step_id == steps - 1)
    def _():
        whole = (total[...] + added).astype(BF16)
        upper_out[...] = whole[:upper_rows]
        lower_out[...] = whole[upper_rows:]


def mixer(projected, taps, prefix, log_gate, regular, out_weight, length):
    rows_total = projected.shape[1]
    heads = regular.shape[0]
    together = 2
    upper_rows = rows_total * 5 // 8
    lower_rows = rows_total - upper_rows
    width = heads * DK
    features = out_weight.shape[1]
    share = prefix.shape[0] // heads

    def columns(part):
        return pl.BlockSpec((1, rows_total, together * DK), lambda step: (part, 0, step))

    return pl.pallas_call(
        functools.partial(mixer_kernel, heads, upper_rows),
        grid=(heads // together,),
        out_shape=(
            jax.ShapeDtypeStruct((upper_rows, features), BF16),
            jax.ShapeDtypeStruct((lower_rows, features), BF16),
            jax.ShapeDtypeStruct((heads, 2, DK, DK), F32),
            jax.ShapeDtypeStruct((CONV - 1, 3, 1, width), F32),
        ),
        in_specs=[
            pl.BlockSpec(memory_space=pltpu.SMEM),
            columns(0),
            columns(1),
            columns(2),
            pl.BlockSpec((3, CONV, together * DK), lambda step: (0, 0, step)),
            pl.BlockSpec(memory_space=pl.ANY),
            pl.BlockSpec((together, 1, rows_total), lambda step: (step, 0, 0)),
            pl.BlockSpec((together, 1, DK), lambda step: (step, 0, 0)),
            pl.BlockSpec((together * DK, features), lambda step: (step, 0)),
        ],
        out_specs=(
            pl.BlockSpec((upper_rows, features), lambda step: (0, 0)),
            pl.BlockSpec((lower_rows, features), lambda step: (0, 0)),
            pl.BlockSpec((together, 2, DK, DK), lambda step: (step, 0, 0, 0)),
            pl.BlockSpec((CONV - 1, 3, 1, together * DK), lambda step: (0, 0, 0, step)),
        ),
        scratch_shapes=[
            pltpu.VMEM((together * 3, rows_total + 8, DK), F32),
            pltpu.VMEM((rows_total, features), F32),
            pltpu.VMEM(prefix.shape, prefix.dtype),
        ],
        compiler_params=pltpu.CompilerParams(
            dimension_semantics=("arbitrary",), vmem_limit_bytes=50 << 20
        ),
        name="mixer",
    )(
        length,
        projected,
        projected,
        projected,
        taps,
        prefix,
        log_gate[:, None, :],
        regular[:, None, :],
        pltpu.with_memory_space_constraint(out_weight, pltpu.HBM),
    )


def on_device(
    tokens,
    norm_gains,
    qkv_weight,
    conv_weight,
    log_decay,
    regular,
    out_weight,
    gate_up_weight,
    down_weight,
    prefix_cache,
    prefix_tail,
    suffix_len,
    request_group,
    prefix_owner,
):
    rows_total, half = tokens.shape
    first = lax.axis_index("tensor") == 0
    packed = pack(
        prefix_cache[0],
        jnp.transpose(prefix_tail, (1, 2, 0, 3)),
        request_group,
        lax.axis_size("dp"),
    )
    packed, tokens = lax.optimization_barrier((packed, tokens))
    theirs = other_core(tokens)
    arrived = lax.all_to_all(packed, "dp", 0, 0)
    whole_rows = jnp.concatenate(
        [jnp.where(first, tokens, theirs), jnp.where(first, theirs, tokens)], axis=1
    ).astype(F32)
    normed = rms_rows(whole_rows, norm_gains[0])
    planes = jnp.transpose(qkv_weight, (1, 0, 2))
    projected = jnp.einsum("rd,jdc->jrc", normed, planes, preferred_element_type=F32)
    arrived, projected, gate_up_weight = lax.optimization_barrier(
        (arrived, projected, gate_up_weight)
    )
    prefix = lax.all_to_all(route(prefix_owner, arrived), "dp", 0, 0)
    prefix, gate_up_matrix = lax.optimization_barrier(
        (prefix, gate_up_weight.reshape(gate_up_weight.shape[0], -1))
    )
    upper, lower, state_out, tail_out = mixer(
        projected,
        jnp.transpose(conv_weight, (1, 0, 2)),
        prefix,
        log_decay[0],
        regular,
        out_weight,
        suffix_len,
    )
    hidden_width = gate_up_matrix.shape[1] // 2
    results = []
    for start, partial in ((0, upper), (upper.shape[0], lower)):
        rows = slice(start, start + partial.shape[0])
        here, there = tokens[rows], theirs[rows]
        before = jnp.concatenate(
            [jnp.where(first, here, there), jnp.where(first, there, here)], axis=1
        ).astype(F32)
        attended = partial.astype(F32) + other_core(partial).astype(F32)
        middle = (before + attended).astype(BF16)
        gate_up = jnp.dot(
            rms_rows(middle.astype(F32), norm_gains[1]), gate_up_matrix, preferred_element_type=F32
        )
        hidden = jax.nn.silu(gate_up[:, :hidden_width]) * gate_up[:, hidden_width:]
        forward = jnp.dot(hidden.astype(BF16), down_weight, preferred_element_type=F32)
        left, right = forward[:, :half], forward[:, half:]
        leaving = other_core(jnp.where(first, right, left).astype(BF16))
        kept = jnp.where(first, left, right) + leaving.astype(F32)
        base = jnp.where(first, middle[:, :half], middle[:, half:]).astype(F32)
        live_rows = jnp.arange(rows.start, rows.stop) < suffix_len[0]
        results.append(jnp.where(live_rows[:, None], base + kept, 0.0).astype(BF16))
    result = jnp.pad(results[0], ((0, results[1].shape[0]), (0, 0)))
    result = lax.dynamic_update_slice(result, results[1], (results[0].shape[0], 0))
    return (result, state_out[None], jnp.transpose(tail_out, (2, 0, 1, 3)))


def solution(mesh):
    return jax.shard_map(
        on_device,
        mesh=mesh,
        in_specs=(
            P("dp", "tensor"),
            P(),
            P(None, None, "tensor"),
            P(None, None, "tensor"),
            P("dp", "tensor", None),
            P("tensor", None),
            P("tensor", None),
            P(None, None, "tensor"),
            P("tensor", None),
            P("dp", "tensor", None, None, None),
            P("dp", None, None, "tensor"),
            P("dp"),
            P("dp"),
            P(),
        ),
        out_specs=(
            P("dp", "tensor"),
            P("dp", "tensor", None, None, None),
            P("dp", None, None, "tensor"),
        ),
        check_vma=False,
    )
```

```python
import functools

import jax
import jax.numpy as jnp
from jax import lax
from jax.experimental import pallas as pl
from jax.experimental.pallas import tpu as pltpu
from jax.sharding import PartitionSpec as P

DK = 128
CONV = 4
BLOCK = 128
ITERS = 4
LANES = 128
BF16 = jnp.bfloat16
F32 = jnp.float32


def rms_rows(floats, gain):
    inverse = lax.rsqrt(jnp.mean(floats * floats, axis=-1, keepdims=True) + 1e-05)
    return (floats * inverse * gain).astype(BF16)


def other_core(array_in):
    return lax.ppermute(array_in, "tensor", [(0, 1), (1, 0)])


def halves(value):
    high = value.astype(BF16)
    return high, (value - high.astype(F32)).astype(BF16)


def dot_nn(left, right):
    return lax.dot_general(left, right, (((1,), (0,)), ((), ())), preferred_element_type=F32)


def dot_nt(left, right):
    return lax.dot_general(left, right, (((1,), (1,)), ((), ())), preferred_element_type=F32)


def dot_tn(left, right):
    return lax.dot_general(left, right, (((0,), (0,)), ((), ())), preferred_element_type=F32)


def pack_kernel(group, cache, tail, packed):
    count, rows, _ = packed.shape
    heads = cache.shape[0]
    share = count // heads
    state_rows = rows - 8
    tail_rows = -(-(CONV - 1) * 3 // share)
    tag = jnp.full((1, LANES), group[0], jnp.int32).astype(F32)
    for head in range(heads):
        lanes = slice(head * DK, (head + 1) * DK)
        for piece in range(share):
            plane, offset = divmod(piece * state_rows, DK)
            parts = [cache[head, plane, offset : offset + state_rows, :]]
            for index in range(piece * tail_rows, (piece + 1) * tail_rows):
                if index < (CONV - 1) * 3:
                    parts.append(tail[index // 3, index % 3, :, lanes])
                else:
                    parts.append(tag)
            parts.append(jnp.broadcast_to(tag, (8 - tail_rows, LANES)))
            packed[head * share + piece] = jnp.concatenate(parts, axis=0).astype(BF16)


def pack(prefix_cache, prefix_tail, request_group, count):
    rows = prefix_cache.shape[0] * 2 * DK // count + 8
    return pl.pallas_call(
        pack_kernel,
        out_shape=jax.ShapeDtypeStruct((count, rows, LANES), BF16),
        in_specs=[
            pl.BlockSpec(memory_space=pltpu.SMEM),
            pl.BlockSpec(memory_space=pltpu.VMEM),
            pl.BlockSpec(memory_space=pltpu.VMEM),
        ],
        out_specs=pl.BlockSpec(memory_space=pltpu.VMEM),
        name="pack",
    )(request_group, prefix_cache, prefix_tail)


def route_kernel(owners, source, target, arrived, leaving):
    pltpu.sync_copy(source, arrived)
    count, rows, _ = arrived.shape
    groups = owners.shape[0]
    held = [arrived[owners[group]].astype(F32) for group in range(groups)]

    def fill(slot, carry):
        wanted = arrived[slot].astype(F32)[rows - 1 : rows, :]
        chosen = held[0]
        for group in range(1, groups):
            chosen = jnp.where(wanted == float(group), held[group], chosen)
        leaving[slot] = chosen.astype(BF16)
        return carry

    lax.fori_loop(0, count, fill, 0)
    pltpu.sync_copy(leaving, target)


def route(prefix_owner, arrived):
    return pl.pallas_call(
        route_kernel,
        out_shape=pltpu.HBM(arrived.shape, arrived.dtype),
        in_specs=[
            pl.BlockSpec(memory_space=pltpu.SMEM),
            pl.BlockSpec(memory_space=pl.ANY),
        ],
        out_specs=pl.BlockSpec(memory_space=pltpu.HBM),
        scratch_shapes=[pltpu.VMEM(arrived.shape, arrived.dtype)] * 2,
        compiler_params=pltpu.CompilerParams(vmem_limit_bytes=8 << 20),
        name="route",
    )(prefix_owner, arrived)


def mixer_kernel(
    heads_total,
    upper_rows,
    length_ref,
    query_in,
    key_in,
    value_in,
    taps,
    prefix_source,
    decay,
    regular,
    out_weight,
    upper_out,
    lower_out,
    state_out,
    tail_out,
    extended,
    total,
    prefix,
):
    rows_total = query_in.shape[1]
    blocks = rows_total // BLOCK
    step_id = pl.program_id(0)
    length = length_ref[0]
    local_heads = regular.shape[0]
    steps = pl.num_programs(0)
    share = prefix_source.shape[0] // heads_total

    @pl.when(step_id == 0)
    def _():
        pltpu.sync_copy(prefix_source, prefix)

    state_rows = prefix.shape[1] - 8
    tail_rows = -(-(CONV - 1) * 3 // share)
    live = lax.broadcasted_iota(jnp.int32, (rows_total, 1), 0) < length
    lane = lax.broadcasted_iota(jnp.int32, (BLOCK, BLOCK), 1)
    row = lax.broadcasted_iota(jnp.int32, (BLOCK, BLOCK), 0)
    causal = row >= lane

    chains = []
    for local in range(local_heads):
        lanes = slice(local * DK, (local + 1) * DK)
        chunks = [
            prefix[(step_id * local_heads + local) * share + piece].astype(F32)
            for piece in range(share)
        ]
        state = jnp.concatenate([chunk[:state_rows] for chunk in chunks], axis=0)
        hstate, gstate = state[:DK], state[DK:]
        activated = []
        for part, source in enumerate((query_in, key_in, value_in)):
            longer = extended.at[local * 3 + part]
            for before in range(CONV - 1):
                piece, inside = divmod(before * 3 + part, tail_rows)
                place = state_rows + inside
                longer[5 + before : 6 + before, :] = chunks[piece][place : place + 1]
            longer[8 : 8 + rows_total, :] = source[0, :, lanes]
            convolved = taps[part, 0:1, lanes] * longer[pl.ds(5, rows_total), :]
            for tap in range(1, CONV):
                convolved = (
                    convolved
                    + taps[part, tap : tap + 1, lanes] * longer[pl.ds(5 + tap, rows_total), :]
                )
            for place in range(CONV - 1):
                tail_out[place, part, :, lanes] = longer[pl.ds(length + 5 + place, 1), :]
            activated.append(convolved / (1.0 + jnp.exp(-convolved)))
        queries, key_rows, value_rows = activated
        queries = queries * lax.rsqrt(jnp.sum(queries * queries, axis=-1, keepdims=True) + 1e-06)
        key_rows = key_rows * lax.rsqrt(
            jnp.sum(key_rows * key_rows, axis=-1, keepdims=True) + 1e-06
        )
        key_rows = jnp.where(live, key_rows, 0.0)
        value_rows = jnp.where(live, value_rows, 0.0)
        for block in range(blocks):
            rows = slice(block * BLOCK, (block + 1) * BLOCK)
            keys, values = key_rows[rows], value_rows[rows]
            gates = decay[local, :, block * BLOCK : (block + 1) * BLOCK]
            position = lax.broadcasted_iota(jnp.int32, (1, BLOCK), 1) + block * BLOCK
            gates = jnp.where(position < length, gates, 0.0)
            down = jnp.sum(jnp.where(causal, gates, 0.0), axis=1, keepdims=True)
            wide = jnp.broadcast_to(down, (BLOCK, BLOCK))
            differ = wide - wide.T
            weights = jnp.where(causal, jnp.exp(jnp.minimum(differ, 0.0)), 0.0)
            growth = jnp.exp(wide)
            last = down[BLOCK - 1 : BLOCK, :]
            root_tail = jnp.exp(0.5 * (last - down))
            decay_last = jnp.exp(last)
            keys_high = keys.astype(BF16)
            mixing = jnp.concatenate([keys.T, hstate], axis=1).astype(BF16)
            chains.append(
                (
                    queries[rows],
                    jnp.concatenate([keys_high, keys_high], axis=0),
                    jnp.concatenate([mixing, mixing], axis=0),
                    gstate.astype(BF16),
                    values.astype(BF16),
                    weights,
                    growth,
                    regular[local],
                )
            )
            grown = jnp.concatenate([keys * root_tail, values * root_tail], axis=1).astype(BF16)
            update = dot_tn(grown, grown[:, :DK])
            hstate = decay_last * hstate + update[:DK]
            gstate = decay_last * gstate + update[DK:]
        state_out[local, 0] = hstate
        state_out[local, 1] = gstate

    count = len(chains)
    search = [chain[0] for chain in chains]
    residual = list(search)
    norm_now = [jnp.sum(r * r, axis=-1, keepdims=True) for r in residual]
    everyone = range(count)
    for iteration in range(ITERS):
        both = [
            dot_nn(jnp.concatenate(halves(search[index]), axis=1), chains[index][2])
            for index in everyone
        ]
        reach = [both[index][:, :BLOCK] * chains[index][5] for index in everyone]
        near = [
            dot_nn(jnp.concatenate(halves(reach[index]), axis=1), chains[index][1])
            for index in everyone
        ]
        applied = [
            chains[index][6] * both[index][:, BLOCK:]
            + near[index]
            + chains[index][7] * search[index]
            for index in everyone
        ]
        step = [
            norm_now[index] / jnp.sum(search[index] * applied[index], axis=-1, keepdims=True)
            for index in everyone
        ]
        if iteration == 0:
            solved = [step[index] * search[index] for index in everyone]
            correlated = [step[index] * reach[index] for index in everyone]
        else:
            solved = [solved[index] + step[index] * search[index] for index in everyone]
            correlated = [correlated[index] + step[index] * reach[index] for index in everyone]
        if iteration < ITERS - 1:
            residual = [residual[index] - step[index] * applied[index] for index in everyone]
            norm_next = [jnp.sum(r * r, axis=-1, keepdims=True) for r in residual]
            search = [
                residual[index] + norm_next[index] / norm_now[index] * search[index]
                for index in everyone
            ]
            norm_now = norm_next
    outputs = []
    for index in range(count):
        _, _, _, g_high, v_high, _, growth, _ = chains[index]
        recall = dot_nt((growth * solved[index]).astype(BF16), g_high)
        outputs.append((recall + dot_nn(correlated[index].astype(BF16), v_high)).astype(BF16))
    heads_out = jnp.concatenate(
        [
            jnp.concatenate(outputs[local * blocks : (local + 1) * blocks], axis=0)
            for local in range(local_heads)
        ],
        axis=1,
    )
    added = dot_nn(heads_out, out_weight[...])

    @pl.when(step_id == 0)
    def _():
        total[...] = added

    @pl.when((step_id > 0) & (step_id < steps - 1))
    def _():
        total[...] += added

    @pl.when(step_id == steps - 1)
    def _():
        whole = (total[...] + added).astype(BF16)
        upper_out[...] = whole[:upper_rows]
        lower_out[...] = whole[upper_rows:]


def mixer(projected, taps, prefix, log_gate, regular, out_weight, length):
    rows_total = projected.shape[1]
    heads = regular.shape[0]
    together = 2
    upper_rows = rows_total * 5 // 8
    lower_rows = rows_total - upper_rows
    width = heads * DK
    features = out_weight.shape[1]
    share = prefix.shape[0] // heads

    def columns(part):
        return pl.BlockSpec((1, rows_total, together * DK), lambda step: (part, 0, step))

    return pl.pallas_call(
        functools.partial(mixer_kernel, heads, upper_rows),
        grid=(heads // together,),
        out_shape=(
            jax.ShapeDtypeStruct((upper_rows, features), BF16),
            jax.ShapeDtypeStruct((lower_rows, features), BF16),
            jax.ShapeDtypeStruct((heads, 2, DK, DK), F32),
            jax.ShapeDtypeStruct((CONV - 1, 3, 1, width), F32),
        ),
        in_specs=[
            pl.BlockSpec(memory_space=pltpu.SMEM),
            columns(0),
            columns(1),
            columns(2),
            pl.BlockSpec((3, CONV, together * DK), lambda step: (0, 0, step)),
            pl.BlockSpec(memory_space=pl.ANY),
            pl.BlockSpec((together, 1, rows_total), lambda step: (step, 0, 0)),
            pl.BlockSpec((together, 1, DK), lambda step: (step, 0, 0)),
            pl.BlockSpec((together * DK, features), lambda step: (step, 0)),
        ],
        out_specs=(
            pl.BlockSpec((upper_rows, features), lambda step: (0, 0)),
            pl.BlockSpec((lower_rows, features), lambda step: (0, 0)),
            pl.BlockSpec((together, 2, DK, DK), lambda step: (step, 0, 0, 0)),
            pl.BlockSpec((CONV - 1, 3, 1, together * DK), lambda step: (0, 0, 0, step)),
        ),
        scratch_shapes=[
            pltpu.VMEM((together * 3, rows_total + 8, DK), F32),
            pltpu.VMEM((rows_total, features), F32),
            pltpu.VMEM(prefix.shape, prefix.dtype),
        ],
        compiler_params=pltpu.CompilerParams(
            dimension_semantics=("arbitrary",), vmem_limit_bytes=50 << 20
        ),
        name="mixer",
    )(
        length,
        projected,
        projected,
        projected,
        taps,
        prefix,
        log_gate[:, None, :],
        regular[:, None, :],
        pltpu.with_memory_space_constraint(out_weight, pltpu.HBM),
    )


def on_device(
    tokens,
    norm_gains,
    qkv_weight,
    conv_weight,
    log_decay,
    regular,
    out_weight,
    gate_up_weight,
    down_weight,
    prefix_cache,
    prefix_tail,
    suffix_len,
    request_group,
    prefix_owner,
):
    rows_total, half = tokens.shape
    first = lax.axis_index("tensor") == 0
    packed = pack(
        prefix_cache[0],
        jnp.transpose(prefix_tail, (1, 2, 0, 3)),
        request_group,
        lax.axis_size("dp"),
    )
    packed, tokens = lax.optimization_barrier((packed, tokens))
    theirs = other_core(tokens)
    arrived = lax.all_to_all(packed, "dp", 0, 0)
    whole_rows = jnp.concatenate(
        [jnp.where(first, tokens, theirs), jnp.where(first, theirs, tokens)], axis=1
    )
    normed = rms_rows(whole_rows.astype(F32), norm_gains[0])
    planes = jnp.transpose(qkv_weight, (1, 0, 2))
    projected = jnp.einsum("rd,jdc->jrc", normed, planes, preferred_element_type=F32)
    arrived, projected, whole_rows, gate_up_weight = lax.optimization_barrier(
        (arrived, projected, whole_rows, gate_up_weight)
    )
    prefix = lax.all_to_all(route(prefix_owner, arrived), "dp", 0, 0)
    prefix, gate_up_matrix = lax.optimization_barrier(
        (prefix, gate_up_weight.reshape(gate_up_weight.shape[0], -1))
    )
    upper, lower, state_out, tail_out = mixer(
        projected,
        jnp.transpose(conv_weight, (1, 0, 2)),
        prefix,
        log_decay[0],
        regular,
        out_weight,
        suffix_len,
    )
    hidden_width = gate_up_matrix.shape[1] // 2
    results = []
    for start, partial in ((0, upper), (upper.shape[0], lower)):
        rows = slice(start, start + partial.shape[0])
        before = whole_rows[rows].astype(F32)
        attended = partial.astype(F32) + other_core(partial).astype(F32)
        middle = (before + attended).astype(BF16)
        gate_up = jnp.dot(
            rms_rows(middle.astype(F32), norm_gains[1]), gate_up_matrix, preferred_element_type=F32
        )
        hidden = jax.nn.silu(gate_up[:, :hidden_width]) * gate_up[:, hidden_width:]
        forward = jnp.dot(hidden.astype(BF16), down_weight, preferred_element_type=F32)
        left, right = forward[:, :half], forward[:, half:]
        leaving = other_core(jnp.where(first, right, left).astype(BF16))
        kept = jnp.where(first, left, right) + leaving.astype(F32)
        base = jnp.where(first, middle[:, :half], middle[:, half:]).astype(F32)
        live_rows = jnp.arange(rows.start, rows.stop) < suffix_len[0]
        results.append(jnp.where(live_rows[:, None], base + kept, 0.0).astype(BF16))
    result = jnp.pad(results[0], ((0, results[1].shape[0]), (0, 0)))
    result = lax.dynamic_update_slice(result, results[1], (results[0].shape[0], 0))
    return (result, state_out[None], jnp.transpose(tail_out, (2, 0, 1, 3)))


def solution(mesh):
    return jax.shard_map(
        on_device,
        mesh=mesh,
        in_specs=(
            P("dp", "tensor"),
            P(),
            P(None, None, "tensor"),
            P(None, None, "tensor"),
            P("dp", "tensor", None),
            P("tensor", None),
            P("tensor", None),
            P(None, None, "tensor"),
            P("tensor", None),
            P("dp", "tensor", None, None, None),
            P("dp", None, None, "tensor"),
            P("dp"),
            P("dp"),
            P(),
        ),
        out_specs=(
            P("dp", "tensor"),
            P("dp", "tensor", None, None, None),
            P("dp", None, None, "tensor"),
        ),
        check_vma=False,
    )
```

```python
import functools

import jax
import jax.numpy as jnp
from jax import lax
from jax.experimental import pallas as pl
from jax.experimental.pallas import tpu as pltpu
from jax.sharding import PartitionSpec as P

DK = 128
CONV = 4
BLOCK = 128
ITERS = 4
LANES = 128
BF16 = jnp.bfloat16
F32 = jnp.float32


def rms_rows(floats, gain):
    inverse = lax.rsqrt(jnp.mean(floats * floats, axis=-1, keepdims=True) + 1e-05)
    return (floats * inverse * gain).astype(BF16)


def other_core(array_in):
    return lax.ppermute(array_in, "tensor", [(0, 1), (1, 0)])


def halves(value):
    high = value.astype(BF16)
    return high, (value - high.astype(F32)).astype(BF16)


def dot_nn(left, right):
    return lax.dot_general(left, right, (((1,), (0,)), ((), ())), preferred_element_type=F32)


def dot_nt(left, right):
    return lax.dot_general(left, right, (((1,), (1,)), ((), ())), preferred_element_type=F32)


def dot_tn(left, right):
    return lax.dot_general(left, right, (((0,), (0,)), ((), ())), preferred_element_type=F32)


def pack_kernel(group, cache, tail, packed):
    count, rows, _ = packed.shape
    heads = cache.shape[0]
    share = count // heads
    state_rows = rows - 8
    tail_rows = -(-(CONV - 1) * 3 // share)
    tag = jnp.full((1, LANES), group[0], jnp.int32).astype(F32)
    for head in range(heads):
        lanes = slice(head * DK, (head + 1) * DK)
        for piece in range(share):
            plane, offset = divmod(piece * state_rows, DK)
            parts = [cache[head, plane, offset : offset + state_rows, :]]
            for index in range(piece * tail_rows, (piece + 1) * tail_rows):
                if index < (CONV - 1) * 3:
                    parts.append(tail[index // 3, index % 3, :, lanes])
                else:
                    parts.append(tag)
            parts.append(jnp.broadcast_to(tag, (8 - tail_rows, LANES)))
            packed[head * share + piece] = jnp.concatenate(parts, axis=0).astype(BF16)


def pack(prefix_cache, prefix_tail, request_group, count):
    rows = prefix_cache.shape[0] * 2 * DK // count + 8
    return pl.pallas_call(
        pack_kernel,
        out_shape=jax.ShapeDtypeStruct((count, rows, LANES), BF16),
        in_specs=[
            pl.BlockSpec(memory_space=pltpu.SMEM),
            pl.BlockSpec(memory_space=pltpu.VMEM),
            pl.BlockSpec(memory_space=pltpu.VMEM),
        ],
        out_specs=pl.BlockSpec(memory_space=pltpu.VMEM),
        name="pack",
    )(request_group, prefix_cache, prefix_tail)


def route_kernel(owners, source, target, arrived, leaving):
    pltpu.sync_copy(source, arrived)
    count, rows, _ = arrived.shape
    groups = owners.shape[0]
    held = [arrived[owners[group]].astype(F32) for group in range(groups)]

    def fill(slot, carry):
        wanted = arrived[slot].astype(F32)[rows - 1 : rows, :]
        chosen = held[0]
        for group in range(1, groups):
            chosen = jnp.where(wanted == float(group), held[group], chosen)
        leaving[slot] = chosen.astype(BF16)
        return carry

    lax.fori_loop(0, count, fill, 0, unroll=8)
    pltpu.sync_copy(leaving, target)


def route(prefix_owner, arrived):
    return pl.pallas_call(
        route_kernel,
        out_shape=pltpu.HBM(arrived.shape, arrived.dtype),
        in_specs=[
            pl.BlockSpec(memory_space=pltpu.SMEM),
            pl.BlockSpec(memory_space=pl.ANY),
        ],
        out_specs=pl.BlockSpec(memory_space=pltpu.HBM),
        scratch_shapes=[pltpu.VMEM(arrived.shape, arrived.dtype)] * 2,
        compiler_params=pltpu.CompilerParams(vmem_limit_bytes=8 << 20),
        name="route",
    )(prefix_owner, arrived)


def mixer_kernel(
    heads_total,
    upper_rows,
    length_ref,
    query_in,
    key_in,
    value_in,
    taps,
    prefix_source,
    decay,
    regular,
    out_weight,
    upper_out,
    lower_out,
    state_out,
    tail_out,
    extended,
    total,
    prefix,
):
    rows_total = query_in.shape[1]
    blocks = rows_total // BLOCK
    step_id = pl.program_id(0)
    length = length_ref[0]
    local_heads = regular.shape[0]
    steps = pl.num_programs(0)
    share = prefix_source.shape[0] // heads_total

    @pl.when(step_id == 0)
    def _():
        pltpu.sync_copy(prefix_source, prefix)

    state_rows = prefix.shape[1] - 8
    tail_rows = -(-(CONV - 1) * 3 // share)
    live = lax.broadcasted_iota(jnp.int32, (rows_total, 1), 0) < length
    lane = lax.broadcasted_iota(jnp.int32, (BLOCK, BLOCK), 1)
    row = lax.broadcasted_iota(jnp.int32, (BLOCK, BLOCK), 0)
    causal = row >= lane

    chains = []
    for local in range(local_heads):
        lanes = slice(local * DK, (local + 1) * DK)
        chunks = [
            prefix[(step_id * local_heads + local) * share + piece].astype(F32)
            for piece in range(share)
        ]
        state = jnp.concatenate([chunk[:state_rows] for chunk in chunks], axis=0)
        hstate, gstate = state[:DK], state[DK:]
        activated = []
        for part, source in enumerate((query_in, key_in, value_in)):
            longer = extended.at[local * 3 + part]
            for before in range(CONV - 1):
                piece, inside = divmod(before * 3 + part, tail_rows)
                place = state_rows + inside
                longer[5 + before : 6 + before, :] = chunks[piece][place : place + 1]
            longer[8 : 8 + rows_total, :] = source[0, :, lanes]
            convolved = taps[part, 0:1, lanes] * longer[pl.ds(5, rows_total), :]
            for tap in range(1, CONV):
                convolved = (
                    convolved
                    + taps[part, tap : tap + 1, lanes] * longer[pl.ds(5 + tap, rows_total), :]
                )
            for place in range(CONV - 1):
                tail_out[place, part, :, lanes] = longer[pl.ds(length + 5 + place, 1), :]
            activated.append(convolved / (1.0 + jnp.exp(-convolved)))
        queries, key_rows, value_rows = activated
        queries = queries * lax.rsqrt(jnp.sum(queries * queries, axis=-1, keepdims=True) + 1e-06)
        key_rows = key_rows * lax.rsqrt(
            jnp.sum(key_rows * key_rows, axis=-1, keepdims=True) + 1e-06
        )
        key_rows = jnp.where(live, key_rows, 0.0)
        value_rows = jnp.where(live, value_rows, 0.0)
        for block in range(blocks):
            rows = slice(block * BLOCK, (block + 1) * BLOCK)
            keys, values = key_rows[rows], value_rows[rows]
            gates = decay[local, :, block * BLOCK : (block + 1) * BLOCK]
            position = lax.broadcasted_iota(jnp.int32, (1, BLOCK), 1) + block * BLOCK
            gates = jnp.where(position < length, gates, 0.0)
            down = jnp.sum(jnp.where(causal, gates, 0.0), axis=1, keepdims=True)
            wide = jnp.broadcast_to(down, (BLOCK, BLOCK))
            differ = wide - wide.T
            weights = jnp.where(causal, jnp.exp(jnp.minimum(differ, 0.0)), 0.0)
            growth = jnp.exp(wide)
            last = down[BLOCK - 1 : BLOCK, :]
            root_tail = jnp.exp(0.5 * (last - down))
            decay_last = jnp.exp(last)
            keys_high = keys.astype(BF16)
            mixing = jnp.concatenate([keys.T, hstate], axis=1).astype(BF16)
            chains.append(
                (
                    queries[rows],
                    jnp.concatenate([keys_high, keys_high], axis=0),
                    jnp.concatenate([mixing, mixing], axis=0),
                    gstate.astype(BF16),
                    values.astype(BF16),
                    weights,
                    growth,
                    regular[local],
                )
            )
            grown = jnp.concatenate([keys * root_tail, values * root_tail], axis=1).astype(BF16)
            update = dot_tn(grown, grown[:, :DK])
            hstate = decay_last * hstate + update[:DK]
            gstate = decay_last * gstate + update[DK:]
        state_out[local, 0] = hstate
        state_out[local, 1] = gstate

    count = len(chains)
    search = [chain[0] for chain in chains]
    residual = list(search)
    norm_now = [jnp.sum(r * r, axis=-1, keepdims=True) for r in residual]
    everyone = range(count)
    for iteration in range(ITERS):
        both = [
            dot_nn(jnp.concatenate(halves(search[index]), axis=1), chains[index][2])
            for index in everyone
        ]
        reach = [both[index][:, :BLOCK] * chains[index][5] for index in everyone]
        near = [
            dot_nn(jnp.concatenate(halves(reach[index]), axis=1), chains[index][1])
            for index in everyone
        ]
        applied = [
            chains[index][6] * both[index][:, BLOCK:]
            + near[index]
            + chains[index][7] * search[index]
            for index in everyone
        ]
        step = [
            norm_now[index] / jnp.sum(search[index] * applied[index], axis=-1, keepdims=True)
            for index in everyone
        ]
        if iteration == 0:
            solved = [step[index] * search[index] for index in everyone]
            correlated = [step[index] * reach[index] for index in everyone]
        else:
            solved = [solved[index] + step[index] * search[index] for index in everyone]
            correlated = [correlated[index] + step[index] * reach[index] for index in everyone]
        if iteration < ITERS - 1:
            residual = [residual[index] - step[index] * applied[index] for index in everyone]
            norm_next = [jnp.sum(r * r, axis=-1, keepdims=True) for r in residual]
            search = [
                residual[index] + norm_next[index] / norm_now[index] * search[index]
                for index in everyone
            ]
            norm_now = norm_next
    outputs = []
    for index in range(count):
        _, _, _, g_high, v_high, _, growth, _ = chains[index]
        recall = dot_nt((growth * solved[index]).astype(BF16), g_high)
        outputs.append((recall + dot_nn(correlated[index].astype(BF16), v_high)).astype(BF16))
    heads_out = jnp.concatenate(
        [
            jnp.concatenate(outputs[local * blocks : (local + 1) * blocks], axis=0)
            for local in range(local_heads)
        ],
        axis=1,
    )
    added = dot_nn(heads_out, out_weight[...])

    @pl.when(step_id == 0)
    def _():
        total[...] = added

    @pl.when((step_id > 0) & (step_id < steps - 1))
    def _():
        total[...] += added

    @pl.when(step_id == steps - 1)
    def _():
        whole = (total[...] + added).astype(BF16)
        upper_out[...] = whole[:upper_rows]
        lower_out[...] = whole[upper_rows:]


def mixer(projected, taps, prefix, log_gate, regular, out_weight, length):
    rows_total = projected.shape[1]
    heads = regular.shape[0]
    together = 2
    upper_rows = rows_total * 5 // 8
    lower_rows = rows_total - upper_rows
    width = heads * DK
    features = out_weight.shape[1]
    share = prefix.shape[0] // heads

    def columns(part):
        return pl.BlockSpec((1, rows_total, together * DK), lambda step: (part, 0, step))

    return pl.pallas_call(
        functools.partial(mixer_kernel, heads, upper_rows),
        grid=(heads // together,),
        out_shape=(
            jax.ShapeDtypeStruct((upper_rows, features), BF16),
            jax.ShapeDtypeStruct((lower_rows, features), BF16),
            jax.ShapeDtypeStruct((heads, 2, DK, DK), F32),
            jax.ShapeDtypeStruct((CONV - 1, 3, 1, width), F32),
        ),
        in_specs=[
            pl.BlockSpec(memory_space=pltpu.SMEM),
            columns(0),
            columns(1),
            columns(2),
            pl.BlockSpec((3, CONV, together * DK), lambda step: (0, 0, step)),
            pl.BlockSpec(memory_space=pl.ANY),
            pl.BlockSpec((together, 1, rows_total), lambda step: (step, 0, 0)),
            pl.BlockSpec((together, 1, DK), lambda step: (step, 0, 0)),
            pl.BlockSpec((together * DK, features), lambda step: (step, 0)),
        ],
        out_specs=(
            pl.BlockSpec((upper_rows, features), lambda step: (0, 0)),
            pl.BlockSpec((lower_rows, features), lambda step: (0, 0)),
            pl.BlockSpec((together, 2, DK, DK), lambda step: (step, 0, 0, 0)),
            pl.BlockSpec((CONV - 1, 3, 1, together * DK), lambda step: (0, 0, 0, step)),
        ),
        scratch_shapes=[
            pltpu.VMEM((together * 3, rows_total + 8, DK), F32),
            pltpu.VMEM((rows_total, features), F32),
            pltpu.VMEM(prefix.shape, prefix.dtype),
        ],
        compiler_params=pltpu.CompilerParams(
            dimension_semantics=("arbitrary",), vmem_limit_bytes=50 << 20
        ),
        name="mixer",
    )(
        length,
        projected,
        projected,
        projected,
        taps,
        prefix,
        log_gate[:, None, :],
        regular[:, None, :],
        pltpu.with_memory_space_constraint(out_weight, pltpu.HBM),
    )


def on_device(
    tokens,
    norm_gains,
    qkv_weight,
    conv_weight,
    log_decay,
    regular,
    out_weight,
    gate_up_weight,
    down_weight,
    prefix_cache,
    prefix_tail,
    suffix_len,
    request_group,
    prefix_owner,
):
    rows_total, half = tokens.shape
    first = lax.axis_index("tensor") == 0
    packed = pack(
        prefix_cache[0],
        jnp.transpose(prefix_tail, (1, 2, 0, 3)),
        request_group,
        lax.axis_size("dp"),
    )
    packed, tokens = lax.optimization_barrier((packed, tokens))
    theirs = other_core(tokens)
    arrived = lax.all_to_all(packed, "dp", 0, 0)
    whole_rows = jnp.concatenate(
        [jnp.where(first, tokens, theirs), jnp.where(first, theirs, tokens)], axis=1
    )
    normed = rms_rows(whole_rows.astype(F32), norm_gains[0])
    planes = jnp.transpose(qkv_weight, (1, 0, 2))
    projected = jnp.einsum("rd,jdc->jrc", normed, planes, preferred_element_type=F32)
    arrived, projected, whole_rows, gate_up_weight = lax.optimization_barrier(
        (arrived, projected, whole_rows, gate_up_weight)
    )
    prefix = lax.all_to_all(route(prefix_owner, arrived), "dp", 0, 0)
    prefix, gate_up_matrix = lax.optimization_barrier(
        (prefix, gate_up_weight.reshape(gate_up_weight.shape[0], -1))
    )
    upper, lower, state_out, tail_out = mixer(
        projected,
        jnp.transpose(conv_weight, (1, 0, 2)),
        prefix,
        log_decay[0],
        regular,
        out_weight,
        suffix_len,
    )
    hidden_width = gate_up_matrix.shape[1] // 2
    results = []
    for start, partial in ((0, upper), (upper.shape[0], lower)):
        rows = slice(start, start + partial.shape[0])
        before = whole_rows[rows].astype(F32)
        attended = partial.astype(F32) + other_core(partial).astype(F32)
        middle = (before + attended).astype(BF16)
        gate_up = jnp.dot(
            rms_rows(middle.astype(F32), norm_gains[1]), gate_up_matrix, preferred_element_type=F32
        )
        hidden = jax.nn.silu(gate_up[:, :hidden_width]) * gate_up[:, hidden_width:]
        forward = jnp.dot(hidden.astype(BF16), down_weight, preferred_element_type=F32)
        left, right = forward[:, :half], forward[:, half:]
        leaving = other_core(jnp.where(first, right, left).astype(BF16))
        kept = jnp.where(first, left, right) + leaving.astype(F32)
        base = jnp.where(first, middle[:, :half], middle[:, half:]).astype(F32)
        live_rows = jnp.arange(rows.start, rows.stop) < suffix_len[0]
        results.append(jnp.where(live_rows[:, None], base + kept, 0.0).astype(BF16))
    result = jnp.pad(results[1], ((results[0].shape[0], 0), (0, 0)))
    result = lax.optimization_barrier(result)
    result = lax.dynamic_update_slice(result, results[0], (0, 0))
    return (result, state_out[None], jnp.transpose(tail_out, (2, 0, 1, 3)))


def solution(mesh):
    return jax.shard_map(
        on_device,
        mesh=mesh,
        in_specs=(
            P("dp", "tensor"),
            P(),
            P(None, None, "tensor"),
            P(None, None, "tensor"),
            P("dp", "tensor", None),
            P("tensor", None),
            P("tensor", None),
            P(None, None, "tensor"),
            P("tensor", None),
            P("dp", "tensor", None, None, None),
            P("dp", None, None, "tensor"),
            P("dp"),
            P("dp"),
            P(),
        ),
        out_specs=(
            P("dp", "tensor"),
            P("dp", "tensor", None, None, None),
            P("dp", None, None, "tensor"),
        ),
        check_vma=False,
    )
```
